32 devices in a mesh: dp: 8 (over y, x, core), group: 4 (over z).
Axes of the slice: x: 2, y: 2, z: 4, core: 2. Of those that a mesh axis runs over, the one named last changes fastest.
Arguments:
- tokens: bfloat16 [8192, 2048], P('dp', 'group'), may hold values from -6 to 6
- gate_w: bfloat16 [2048, 1024], P('dp', 'group'), may hold values from -0.125 to 0.125
- up_w: bfloat16 [2048, 1024], P('dp', 'group'), may hold values from -0.125 to 0.125
- block_rows: int32 [32, 128], P('dp'), may hold values from 0 to 1023, as said below
- block_count: int32 [8], P('dp'), may hold values from 1 to 4, as said below
- route_gate: float32 [32, 128], P('dp'), may hold values from 0.05 to 1
- grad_hidden: bfloat16 [4096, 1024], P('dp', 'group'), may hold values from -6 to 6
Outputs:
- hidden: bfloat16 [4096, 1024], P('dp', 'group')
- grad_tokens: bfloat16 [8192, 2048], P('dp', 'group')
- grad_gate_w: float32 [2048, 1024], P('dp', 'group')
- grad_up_w: float32 [2048, 1024], P('dp', 'group')
The draws below stay inside these ranges and needn't reach their ends.
Inputs may be any that keep to these rules, and one draw needn't show every extreme that they name: `block_rows`: the rows of one index of dp name 512 distinct tokens of its own 1024. The live slots of an index of dp are its first block_count ones; some index has all 4 live in every draw.
All inputs are finite; a program needn't handle non-finite values.
Results may differ from the reference program's by a relative error of at most 0.0049.
Values may be sent and summed in bfloat16 or wider, within the bound.
A program may use at most 64 MiB of HBM per device.

```python
import math
import jax
import jax.numpy as jnp
from jax import lax

D = 2048
FF = 1024
BLK = 128
NB = 4
TOK_DEV = 1024
TOKENS = 8192
BLOCKS = 32
ROUTED = 4096
N_DP = 8


def pick_rows(device_key):
    return jax.random.permutation(device_key, TOK_DEV)[:NB * BLK]


def draw_block_rows(key, part):
    holders = TOKENS // TOK_DEV
    device_keys = jax.random.split(key, holders)
    picked = jax.vmap(pick_rows)(device_keys)
    return picked.reshape(holders * NB, BLK).astype(jnp.int32)


def draw_block_count(key, part):
    holders = TOKENS // TOK_DEV
    key_one, key_two = jax.random.split(jax.random.fold_in(key, 7))
    counts = jax.random.randint(key_one, (holders,), 1, NB + 1)
    chosen = jax.random.randint(key_two, (), 0, holders)
    return jnp.where(jnp.arange(holders) == chosen, NB, counts).astype(jnp.int32)


def spiked(result, own_key, source, target, shards_of, factor):
    def block_of(axis_at):
        return (jnp.arange(result.shape[axis_at]) // (result.shape[axis_at] // shards_of)).reshape((-1,) + (1,) * (result.ndim - 1 - axis_at))

    first = jax.random.permutation(own_key, shards_of)[block_of(target)]
    far = (block_of(target) + shards_of // 2) % shards_of
    return jnp.where((block_of(source) == first) | (block_of(source) == far), factor * result, result)


def block_levels(rng, extent, cuts, least, high):
    gain, own = 1.0, jax.random.fold_in(rng, 6)
    for axis_at, blocks in cuts:
        draws = jnp.exp(jax.random.uniform(jax.random.fold_in(own, axis_at), (blocks,), jnp.float32, least / len(cuts), high / len(cuts)))
        gain = gain * jnp.repeat(draws, extent[axis_at] // blocks).reshape([-1 if axis == axis_at else 1 for axis in range(len(extent))])
    return gain


def noise(own_key, shape, width, most, shards=(), kind=jnp.bfloat16):
    drawn = jax.random.normal(own_key, shape, jnp.float32) * width
    if len(shards) > 0:
        drawn = block_levels(own_key, shape, shards, -0.22, 0.18) * drawn
    return jnp.clip(drawn, min=-most, max=most).astype(kind)


def bell_draw_with(own_key, shape, spread, limit, cuts, heavy, held_as=jnp.bfloat16):
    entries = spread * jax.random.normal(own_key, shape, jnp.float32)
    if cuts:
        entries = entries * block_levels(own_key, shape, cuts, -0.22, 0.18)
    return jnp.clip(spiked(entries, jax.random.fold_in(own_key, 3), *heavy), -limit, limit).astype(held_as)


def setup_inputs(seed: int = 0) -> dict:
    key_list = jax.random.split(jax.random.key(seed), 8)
    return {
        "tokens": bell_draw_with(key_list[0], (TOKENS, D), 1.0, 6.0, ((0, 8), (1, 4)), (0, 1, 8, 2.0)),
        "gate_w": noise(key_list[1], (D, FF), D ** -0.5, 0.125, ((0, 8), (1, 4))),
        "up_w": noise(key_list[2], (D, FF), D ** -0.5, 0.125, ((0, 8), (1, 4))),
        "block_rows": draw_block_rows(jax.random.fold_in(key_list[7], 71), 0),
        "block_count": draw_block_count(jax.random.fold_in(key_list[7], 71), 0),
        "route_gate": jnp.clip(jnp.exp(math.log(1.0) - 2.9957323 * jax.random.uniform(key_list[5], (BLOCKS, BLK), jnp.float32) ** block_levels(key_list[5], (BLOCKS, BLK), ((0, 8),), -0.2, 0.2)), 0.05, 1.0),
        "grad_hidden": noise(key_list[6], (ROUTED, FF), 1.0, 6.0, ((0, 8), (1, 4))),
    }


def reference(tokens, gate_w, up_w, block_rows, block_count, route_gate, grad_hidden):
    routed_len = NB * BLK
    token_sets = tokens.reshape(N_DP, TOK_DEV, D)
    row_sets = block_rows.reshape(N_DP, routed_len)
    gate_sets = route_gate.reshape(N_DP, routed_len)
    grad_sets = grad_hidden.reshape(N_DP, routed_len, FF)

    def device_step(carry, item):
        token_rows, row_index, route_weight, grad_in, live_count = item
        routed = jnp.take(token_rows, row_index, axis=0)
        live = ((jnp.arange(routed_len) // BLK) < live_count).astype(jnp.float32)
        coef = (route_weight * live)[:, None]
        gate_act = jnp.dot(routed, gate_w, preferred_element_type=jnp.float32)
        up_act = jnp.dot(routed, up_w, preferred_element_type=jnp.float32)
        sig = jax.nn.sigmoid(gate_act)
        hidden = (coef * gate_act * sig * up_act).astype(jnp.bfloat16)
        scaled = grad_in.astype(jnp.float32) * coef
        grad_gate = (scaled * up_act * sig * (1.0 + gate_act * (1.0 - sig))).astype(jnp.bfloat16)
        grad_up = (scaled * gate_act * sig).astype(jnp.bfloat16)
        grad_rows = jnp.dot(grad_gate, gate_w.T, preferred_element_type=jnp.float32)
        grad_rows = grad_rows + jnp.dot(grad_up, up_w.T, preferred_element_type=jnp.float32)
        grad_tok = jnp.zeros((TOK_DEV, D), jnp.float32).at[row_index].add(grad_rows).astype(jnp.bfloat16)
        dims = (((0,), (0,)), ((), ()))
        new_gate = carry[0] + lax.dot_general(routed, grad_gate, dims, preferred_element_type=jnp.float32)
        new_up = carry[1] + lax.dot_general(routed, grad_up, dims, preferred_element_type=jnp.float32)
        return (new_gate, new_up), (hidden, grad_tok)

    start_sums = (jnp.zeros((D, FF), jnp.float32), jnp.zeros((D, FF), jnp.float32))
    sums, outputs = lax.scan(device_step, start_sums, (token_sets, row_sets, gate_sets, grad_sets, block_count))
    factor = (N_DP * NB * BLK) ** -0.5
    hidden = outputs[0].reshape(N_DP * routed_len, FF)
    grad_tokens = outputs[1].reshape(N_DP * TOK_DEV, D)
    return hidden, grad_tokens, sums[0] * factor, sums[1] * factor
```

```python
import functools

import jax
import jax.numpy as jnp
from jax import lax
from jax.experimental import pallas as pl
from jax.experimental.pallas import tpu as pltpu
from jax.sharding import PartitionSpec as P

F32 = jnp.float32
BF16 = jnp.bfloat16
CUTS = 1
AHEAD = 3
HOP = 1
DELAY = 1
BOTH = (((0,), (0,)), ((), ()))
BACK = (((1,), (1,)), ((), ()))


def scattered(bits, number):
    return sum(((number >> at) & 1) << bit for at, bit in enumerate(bits))


def kernel(
    n_dp,
    n_g,
    factor,
    tokens_in,
    gate_w,
    up_w,
    rows_in,
    count,
    route_in,
    grad_in,
    hidden,
    grad_tokens,
    grad_gate_w,
    grad_up_w,
    tokens,
    rows,
    route,
    grad_hidden,
    onehot,
    coef,
    routed,
    wg,
    wu,
    grads,
    part,
    outgoing,
    from_left,
    from_right,
    landed,
    sum_g,
    sum_u,
    stage_g,
    stage_u,
    got_g,
    got_u,
    own_sem,
    fwd_sem,
    ag_sem,
    w_send,
    w_recv,
    rs_send,
    left_sem,
    right_sem,
    h_send,
    h_recv,
    local_sem,
):
    n_blocks, block_len = rows.shape
    nb, blk = part.shape[0], part.shape[2]
    n_tok, fw = tokens.shape
    w_rows, width = gate_w.shape
    n_bits = n_dp.bit_length() - 1
    p = lax.axis_index("dp")
    z = lax.axis_index("group")

    def bit(k):
        return (p // 2**k) % 2

    def partner(k):
        return p + 2**k - bit(k) * 2 ** (k + 1)

    upper = list(range(1, n_bits))
    order_g = upper + [0]
    order_u = upper[::-1] + [0]

    copies_in = [
        pltpu.make_async_copy(source, dest, local_sem.at[i])
        for i, (source, dest) in enumerate(
            (
                (tokens_in, tokens),
                (rows_in, rows),
                (route_in, route),
                (gate_w, wg.at[pl.ds(p * w_rows, w_rows)]),
                (up_w, wu.at[pl.ds(p * w_rows, w_rows)]),
                (grad_in, grad_hidden),
            )
        )
    ]
    for copy in copies_in:
        copy.start()

    barrier = pltpu.get_barrier_semaphore()
    for k in range(n_bits):
        pl.semaphore_signal(barrier, inc=1, device_id={"dp": partner(k)})

    @pl.when(z > 0)
    def _():
        pl.semaphore_signal(barrier, inc=1, device_id={"group": z - 1})

    @pl.when(z < n_g - 1)
    def _():
        pl.semaphore_signal(barrier, inc=1, device_id={"group": z + 1})

    def pick(b):
        span = slice(b * block_len, (b + 1) * block_len)
        hot = lax.broadcasted_iota(jnp.int32, (n_tok, block_len), 0) == rows[b : b + 1, :]
        hot = jnp.where(hot, 1.0, 0.0).astype(BF16)
        onehot[:, span] = hot
        picked = lax.dot_general(hot, tokens[...], BOTH, preferred_element_type=F32)
        routed[z, span, :] = picked.astype(BF16)

    copies_in[0].wait()
    copies_in[1].wait()
    pick(0)
    sides = jnp.minimum(z, 1) + jnp.minimum(n_g - 1 - z, 1)
    pl.semaphore_wait(barrier, n_bits + sides)

    def weight_copies(which, phase):
        source, dest, order = ((gate_w, wg, order_g), (up_w, wu, order_u))[which]
        k = order[phase]
        done = order[:phase]
        base = p - sum(bit(j) * 2**j for j in done) if done else p
        copies = []
        for i in range(2**phase):
            c = base + scattered(done, i)
            place = dest.at[pl.ds(c * w_rows, w_rows)]
            copies.append(
                pltpu.make_async_remote_copy(
                    src_ref=source if phase == 0 else place,
                    dst_ref=dest.at[pl.ds(p * w_rows, w_rows)] if phase == 0 else place,
                    send_sem=w_send.at[which, phase],
                    recv_sem=w_recv.at[which, phase],
                    device_id={"dp": partner(k)},
                )
            )
        return copies

    def weight_start(phase):
        for which in range(2):
            for copy in weight_copies(which, phase):
                copy.start()

    def weight_wait(phase):
        for which in range(2):
            dest, order = ((wg, order_g), (wu, order_u))[which]
            span = dest.at[pl.ds(0, w_rows * 2**phase)]
            whole = pltpu.make_async_remote_copy(
                src_ref=span,
                dst_ref=span,
                send_sem=w_send.at[which, phase],
                recv_sem=w_recv.at[which, phase],
                device_id={"dp": partner(order[phase])},
            )
            whole.wait()

    def feature_copy(s, b, send_sem, to):
        place = routed.at[s, pl.ds(pl.multiple_of(b * blk, blk), blk)]
        return pltpu.make_async_remote_copy(
            src_ref=place,
            dst_ref=place,
            send_sem=send_sem,
            recv_sem=ag_sem.at[b, s],
            device_id={"group": to},
        )

    def own_left(b):
        return feature_copy(z, b, own_sem.at[b, 0], z - 1)

    def own_right(b):
        return feature_copy(z, b, own_sem.at[b, 1], z + 1)

    def own_start(b):
        @pl.when(z > 0)
        def _():
            own_left(b).start()

        @pl.when(z < n_g - 1)
        def _():
            own_right(b).start()

    def take(b, k):
        @pl.when(z - k >= 0)
        def _():
            feature_copy(z - k, b, fwd_sem.at[b, z - k], z).wait_recv()

            @pl.when(z < n_g - 1)
            def _():
                feature_copy(z - k, b, fwd_sem.at[b, z - k], z + 1).start()

        @pl.when(z + k < n_g)
        def _():
            feature_copy(z + k, b, fwd_sem.at[b, z + k], z).wait_recv()

            @pl.when(z > 0)
            def _():
                feature_copy(z + k, b, fwd_sem.at[b, z + k], z - 1).start()

    weight_start(0)
    cuts = block_len // blk
    for b in range(min(AHEAD, cuts)):
        own_start(b)
    for b in range(1, n_blocks):
        pick(b)
        for at in range(b * cuts, min(AHEAD, (b + 1) * cuts)):
            own_start(at)
    copies_in[2].wait()
    live = lax.broadcasted_iota(jnp.int32, (n_blocks, block_len), 0) < count[0]
    weights = jnp.where(live, route[...], 0.0)
    for b in range(n_blocks):
        turned = jnp.broadcast_to(weights[b : b + 1, :], (block_len, block_len)).T
        coef[b * block_len : (b + 1) * block_len, :] = turned
    for copy in copies_in[3:]:
        copy.wait()

    distance = 1
    for phase in range(n_bits):
        weight_wait(phase)
        if phase + 1 < n_bits:
            weight_start(phase + 1)
        if distance < n_g:
            take(0, distance)
            distance += 1
    for k in range(distance, n_g):
        take(0, k)

    def block_step(b):
        span = pl.ds(pl.multiple_of(b * blk, blk), blk)
        gate = jnp.zeros((blk, width), F32)
        up = jnp.zeros((blk, width), F32)
        for s in range(n_g):
            x = routed[s, span, :]
            gate += jnp.dot(x, wg[s * fw : (s + 1) * fw, :], preferred_element_type=F32)
            up += jnp.dot(x, wu[s * fw : (s + 1) * fw, :], preferred_element_type=F32)
        c = jnp.concatenate([coef[span, :]] * (width // coef.shape[1]), axis=1)
        sig = jax.nn.sigmoid(gate)
        act = gate * sig
        hidden[span, :] = (c * act * up).astype(BF16)
        scaled = grad_hidden[span, :].astype(F32) * c
        gg = (scaled * up * sig * (1.0 + gate * (1.0 - sig))).astype(BF16)
        gu = (scaled * act).astype(BF16)
        grads[span, :width] = gg
        grads[span, width:] = gu
        for d in range(n_g):
            back = lax.dot_general(
                gg, wg[d * fw : (d + 1) * fw, :], BACK, preferred_element_type=F32
            )
            back += lax.dot_general(
                gu, wu[d * fw : (d + 1) * fw, :], BACK, preferred_element_type=F32
            )
            part[b, d] = back

    def row_copy(b, d, right):
        return pltpu.make_async_remote_copy(
            src_ref=outgoing.at[b, d],
            dst_ref=(from_left if right else from_right).at[b, d],
            send_sem=rs_send.at[b, d],
            recv_sem=(left_sem if right else right_sem).at[b, d],
            device_id={"group": z + 1 if right else z - 1},
        )

    def flow_ends(b):
        @pl.when(z == 0)
        def _():
            for d in range(n_g - 1, 0, -1):
                outgoing[b, d] = part[b, d].astype(BF16)
                row_copy(b, d, True).start()

        @pl.when(z == n_g - 1)
        def _():
            for d in range(n_g - 1):
                outgoing[b, d] = part[b, d].astype(BF16)
                row_copy(b, d, False).start()

    def flow_inner(s):
        right_b = s - HOP * (z - 1)

        @pl.when((z > 0) & (z < n_g - 1) & (right_b >= 0) & (right_b < nb))
        def _():
            for k in range(n_g - 1, 0, -1):
                d = z + k

                @pl.when(d < n_g)
                def _():
                    row_copy(right_b, d, True).wait_recv()
                    outgoing[right_b, d] = (
                        part[right_b, d] + from_left[right_b, d].astype(F32)
                    ).astype(BF16)
                    row_copy(right_b, d, True).start()

        left_b = s - HOP * (n_g - 2 - z)

        @pl.when((z > 0) & (z < n_g - 1) & (left_b >= 0) & (left_b < nb))
        def _():
            for k in range(n_g - 1, 0, -1):
                d = z - k

                @pl.when(d >= 0)
                def _():
                    row_copy(left_b, d, False).wait_recv()
                    outgoing[left_b, d] = (
                        part[left_b, d] + from_right[left_b, d].astype(F32)
                    ).astype(BF16)
                    row_copy(left_b, d, False).start()

    def stage(s, carry):
        @pl.when(s + AHEAD < nb)
        def _():
            own_start(s + AHEAD)

        @pl.when(s + 1 < nb)
        def _():
            take(s + 1, 1)

        block_step(s)
        flow_ends(s)

        @pl.when(s + 1 < nb)
        def _():
            for k in range(2, n_g):
                take(s + 1, k)

        @pl.when((s >= DELAY) & (s + 1 < nb))
        def _():
            flow_inner(s - DELAY)

        return carry

    lax.fori_loop(0, nb, stage, 0)

    def weight_grad(s, carry):
        made = lax.dot_general(routed[s], grads[...], BOTH, preferred_element_type=F32)
        at = pl.ds(pl.multiple_of(s * fw, fw), fw)
        sum_g[at, :] = made[:, :width]
        sum_u[at, :] = made[:, width:]
        return carry

    for s in range(n_g):
        weight_grad(s, 0)

    halves = (
        (sum_g, stage_g, got_g, order_g[::-1]),
        (sum_u, stage_u, got_u, order_u[::-1]),
    )

    def half_offset(phase):
        return sum(w_rows * 2 ** (n_bits - 1 - t) for t in range(phase))

    def half_copy(which, phase):
        total, stage_ref, got, order = halves[which]
        span = pl.ds(half_offset(phase), w_rows * 2 ** (n_bits - 1 - phase))
        return pltpu.make_async_remote_copy(
            src_ref=stage_ref.at[span],
            dst_ref=got.at[span],
            send_sem=h_send.at[which, phase],
            recv_sem=h_recv.at[which, phase],
            device_id={"dp": partner(order[phase])},
        )

    def half_places(which, phase, mine):
        order = halves[which][3]
        k = order[phase]
        rest = order[phase + 1 :]
        base = sum(bit(j) * 2**j for j in order[:phase])
        base = base + (bit(k) if mine else 1 - bit(k)) * 2**k
        start = half_offset(phase)
        for i in range(2 ** len(rest)):
            chunk = pl.multiple_of((base + scattered(rest, i)) * w_rows, w_rows)
            at = start + i * w_rows
            yield pl.ds(chunk, w_rows), slice(at, at + w_rows)

    def half_start(phase):
        for which in range(2):
            total, stage_ref, got, order = halves[which]
            for chunk, at in half_places(which, phase, False):
                stage_ref[at, :] = total[chunk, :].astype(BF16)
            half_copy(which, phase).start()

    def half_wait(phase):
        for which in range(2):
            total, stage_ref, got, order = halves[which]
            half_copy(which, phase).wait_recv()
            for chunk, at in half_places(which, phase, True):
                total[chunk, :] += got[at, :].astype(F32)

    half_start(0)
    steps = list(range(nb - 1 - DELAY, nb + HOP * (n_g - 3)))
    share = -(-len(steps) // max(n_bits - 1, 1))
    for phase in range(n_bits):
        half_wait(phase)
        if phase + 1 < n_bits:
            half_start(phase + 1)
        for step in steps[phase * share : (phase + 1) * share]:
            flow_inner(step)

    mine = pl.ds(pl.multiple_of(p * w_rows, w_rows), w_rows)
    grad_gate_w[...] = sum_g[mine, :] * factor
    grad_up_w[...] = sum_u[mine, :] * factor

    for b in range(nb):
        @pl.when(z > 0)
        def _():
            row_copy(b, z, True).wait_recv()

        @pl.when(z < n_g - 1)
        def _():
            row_copy(b, z, False).wait_recv()

        span = slice(b * blk, (b + 1) * blk)

        @pl.when(z == 0)
        def _():
            landed[span, :] = (part[b, z] + from_right[b, z].astype(F32)).astype(BF16)

        @pl.when(z == n_g - 1)
        def _():
            landed[span, :] = (part[b, z] + from_left[b, z].astype(F32)).astype(BF16)

        @pl.when((z > 0) & (z < n_g - 1))
        def _():
            landed[span, :] = (
                part[b, z] + from_left[b, z].astype(F32) + from_right[b, z].astype(F32)
            ).astype(BF16)

    tile = min(n_tok, 256)

    def place(t, carry):
        at = pl.ds(pl.multiple_of(t * tile, tile), tile)
        grad_tokens[at, :] = jnp.dot(
            onehot[at, :], landed[...], preferred_element_type=F32
        ).astype(BF16)
        return carry

    lax.fori_loop(0, n_tok // tile, place, 0)

    def drain(b, carry):
        @pl.when(z > 0)
        def _():
            own_left(b).wait_send()

        @pl.when(z < n_g - 1)
        def _():
            own_right(b).wait_send()

        for s in range(n_g):
            @pl.when(((s < z) & (z < n_g - 1)) | ((s > z) & (z > 0)))
            def _():
                feature_copy(s, b, fwd_sem.at[b, s], z).wait_send()

            @pl.when(s > z)
            def _():
                row_copy(b, s, True).wait_send()

            @pl.when(s < z)
            def _():
                row_copy(b, s, False).wait_send()

        return carry

    lax.fori_loop(0, nb, drain, 0)
    for phase in range(n_bits):
        for which in range(2):
            half_copy(which, phase).wait_send()


def store(*refs):
    sems = refs[-1]
    half = (len(refs) - 1) // 2
    copies = [
        pltpu.make_async_copy(refs[i], refs[half + i], sems.at[i]) for i in range(half)
    ]
    for copy in copies:
        copy.start()
    for copy in copies:
        copy.wait()


def shards(n_dp, n_g, tokens, gate_w, up_w, block_rows, block_count, route_gate, grad_hidden):
    n_blocks, block_len = block_rows.shape
    nb, blk = n_blocks * CUTS, block_len // CUTS
    n_tok, fw = tokens.shape
    w_rows, width = gate_w.shape
    routed_len = nb * blk
    depth = n_dp * w_rows
    n_bits = n_dp.bit_length() - 1
    factor = float((n_dp * routed_len) ** (-0.5))
    dma = pltpu.SemaphoreType.DMA
    vmem = pl.BlockSpec(memory_space=pltpu.VMEM)
    hbm = pl.BlockSpec(memory_space=pltpu.HBM)
    smem = pl.BlockSpec(memory_space=pltpu.SMEM)
    kept = routed_len * width * 2 + n_tok * fw * 2 + 2 * w_rows * width * 4
    made = pl.pallas_call(
        functools.partial(kernel, n_dp, n_g, factor),
        out_shape=(
            pltpu.VMEM((routed_len, width), BF16),
            pltpu.VMEM((n_tok, fw), BF16),
            pltpu.VMEM((w_rows, width), F32),
            pltpu.VMEM((w_rows, width), F32),
        ),
        in_specs=[hbm, hbm, hbm, hbm, smem, hbm, hbm],
        out_specs=(vmem, vmem, vmem, vmem),
        scratch_shapes=[
            pltpu.VMEM((n_tok, fw), BF16),
            pltpu.VMEM((n_blocks, block_len), jnp.int32),
            pltpu.VMEM((n_blocks, block_len), F32),
            pltpu.VMEM((routed_len, width), BF16),
            pltpu.VMEM((n_tok, routed_len), BF16),
            pltpu.VMEM((routed_len, block_len), F32),
            pltpu.VMEM((n_g, routed_len, fw), BF16),
            pltpu.VMEM((depth, width), BF16),
            pltpu.VMEM((depth, width), BF16),
            pltpu.VMEM((routed_len, 2 * width), BF16),
            pltpu.VMEM((nb, n_g, blk, fw), F32),
            pltpu.VMEM((nb, n_g, blk, fw), BF16),
            pltpu.VMEM((nb, n_g, blk, fw), BF16),
            pltpu.VMEM((nb, n_g, blk, fw), BF16),
            pltpu.VMEM((routed_len, fw), BF16),
            pltpu.VMEM((depth, width), F32),
            pltpu.VMEM((depth, width), F32),
            pltpu.VMEM((depth, width), BF16),
            pltpu.VMEM((depth, width), BF16),
            pltpu.VMEM((depth, width), BF16),
            pltpu.VMEM((depth, width), BF16),
            dma((nb, 2)),
            dma((nb, n_g)),
            dma((nb, n_g)),
            dma((2, n_bits)),
            dma((2, n_bits)),
            dma((nb, n_g)),
            dma((nb, n_g)),
            dma((nb, n_g)),
            dma((2, n_bits)),
            dma((2, n_bits)),
            dma((6,)),
        ],
        compiler_params=pltpu.CompilerParams(
            collective_id=0, has_side_effects=True, vmem_limit_bytes=67043328 - kept
        ),
    )(tokens, gate_w, up_w, block_rows, block_count, route_gate, grad_hidden)
    return pl.pallas_call(
        store,
        out_shape=tuple(jax.ShapeDtypeStruct(x.shape, x.dtype) for x in made),
        in_specs=[vmem] * len(made),
        out_specs=(hbm,) * len(made),
        scratch_shapes=[dma((len(made),))],
        compiler_params=pltpu.CompilerParams(vmem_limit_bytes=2**20),
    )(*made)


def solution(mesh):
    return jax.shard_map(
        functools.partial(shards, mesh.shape["dp"], mesh.shape["group"]),
        mesh=mesh,
        in_specs=(
            P("dp", "group"),
            P("dp", "group"),
            P("dp", "group"),
            P("dp", None),
            P("dp"),
            P("dp", None),
            P("dp", "group"),
        ),
        out_specs=(P("dp", "group"), P("dp", "group"), P("dp", "group"), P("dp", "group")),
        check_vma=False,
    )
```

```python
import functools

import jax
import jax.numpy as jnp
from jax import lax
from jax.experimental import pallas as pl
from jax.experimental.pallas import tpu as pltpu
from jax.sharding import PartitionSpec as P

F32 = jnp.float32
BF16 = jnp.bfloat16
CUTS = 2
AHEAD = 3
NEAR = 2
LEAD = 3
HOP = 2
DEFER = 4
BOTH = (((0,), (0,)), ((), ()))
BACK = (((1,), (1,)), ((), ()))


def kernel(
    n_dp,
    n_g,
    factor,
    tokens_in,
    gate_w,
    up_w,
    rows_in,
    count,
    route_in,
    grad_in,
    hidden,
    grad_tokens,
    grad_gate_w,
    grad_up_w,
    tokens,
    rows,
    route,
    grad_hidden,
    onehot,
    coef,
    routed,
    wg,
    wu,
    grads,
    part,
    outgoing,
    from_left,
    from_right,
    landed,
    sum_g,
    sum_u,
    stage_g,
    stage_u,
    got_g,
    got_u,
    own_sem,
    fwd_sem,
    ag_sem,
    w_send,
    w_recv,
    rs_send,
    left_sem,
    right_sem,
    h_send,
    h_recv,
    local_sem,
):
    n_blocks, block_len = rows.shape
    nb, blk = part.shape[0], part.shape[2]
    n_tok, fw = tokens.shape
    w_rows, width = gate_w.shape
    n_bits = n_dp.bit_length() - 1
    p = lax.axis_index("dp")
    z = lax.axis_index("group")

    def bit(k):
        return (p // 2**k) % 2

    def partner(k):
        return p + 2**k - bit(k) * 2 ** (k + 1)

    upper = list(range(1, n_bits))
    orders = (upper + [0], upper[::-1] + [0])
    inner = (z > 0) & (z < n_g - 1)

    def flipped(bits):
        return p + sum((1 - 2 * bit(k)) * 2**k for k in bits)

    copies_in = [
        pltpu.make_async_copy(source, dest, local_sem.at[i])
        for i, (source, dest) in enumerate(
            (
                (tokens_in, tokens),
                (rows_in, rows),
                (route_in, route),
                (gate_w, wg.at[pl.ds(p * w_rows, w_rows)]),
                (up_w, wu.at[pl.ds(p * w_rows, w_rows)]),
                (grad_in, grad_hidden),
            )
        )
    ]
    for copy in copies_in:
        copy.start()

    barrier = pltpu.get_barrier_semaphore()
    for k in range(n_bits):
        pl.semaphore_signal(barrier, inc=1, device_id={"dp": partner(k)})

    @pl.when(z > 0)
    def _():
        pl.semaphore_signal(barrier, inc=1, device_id={"group": z - 1})

    @pl.when(z < n_g - 1)
    def _():
        pl.semaphore_signal(barrier, inc=1, device_id={"group": z + 1})

    def pick(b):
        span = slice(b * block_len, (b + 1) * block_len)
        hot = lax.broadcasted_iota(jnp.int32, (n_tok, block_len), 0) == rows[b : b + 1, :]
        hot = jnp.where(hot, 1.0, 0.0).astype(BF16)
        onehot[:, span] = hot
        picked = lax.dot_general(hot, tokens[...], BOTH, preferred_element_type=F32)
        routed[z, span, :] = picked.astype(BF16)

    copies_in[0].wait()
    copies_in[1].wait()
    pick(0)
    sides = jnp.minimum(z, 1) + jnp.minimum(n_g - 1 - z, 1)
    pl.semaphore_wait(barrier, n_bits + sides)

    def weight_copy(which, phase, group, owner):
        source, dest = ((gate_w, wg), (up_w, wu))[which]
        place = dest.at[pl.ds(pl.multiple_of(owner * w_rows, w_rows), w_rows)]
        return pltpu.make_async_remote_copy(
            src_ref=place if group else source,
            dst_ref=place,
            send_sem=w_send.at[which, phase, group],
            recv_sem=w_recv.at[which, phase, group],
            device_id={"dp": partner(orders[which][phase])},
        )

    def weight_whole(which, phase, group):
        span = (wg, wu)[which].at[pl.ds(0, w_rows * (2 ** (group - 1) if group else 1))]
        return pltpu.make_async_remote_copy(
            src_ref=span,
            dst_ref=span,
            send_sem=w_send.at[which, phase, group],
            recv_sem=w_recv.at[which, phase, group],
            device_id={"dp": partner(orders[which][phase])},
        )

    def weight_own(phase):
        for which in range(2):
            weight_copy(which, phase, 0, p).start()

    def weight_pass(phase, group):
        for which in range(2):
            order = orders[which]
            weight_whole(which, phase, group).wait_recv()
            low = order[: group - 1] if group else []
            for later in range(phase + 1, n_bits):
                for number in range(2 ** len(low)):
                    bits = [order[phase]] + ([order[group - 1]] if group else [])
                    bits += [k for at, k in enumerate(low) if (number >> at) & 1]
                    weight_copy(which, later, phase + 1, flipped(bits)).start()

    def feature_copy(s, b, send_sem, to):
        place = routed.at[s, pl.ds(pl.multiple_of(b * blk, blk), blk)]
        return pltpu.make_async_remote_copy(
            src_ref=place,
            dst_ref=place,
            send_sem=send_sem,
            recv_sem=ag_sem.at[b, s],
            device_id={"group": to},
        )

    def own_left(b):
        return feature_copy(z, b, own_sem.at[b, 0], z - 1)

    def own_right(b):
        return feature_copy(z, b, own_sem.at[b, 1], z + 1)

    def own_start(b):
        @pl.when(z > 0)
        def _():
            own_left(b).start()

        @pl.when(z < n_g - 1)
        def _():
            own_right(b).start()

    def take(b, k):
        @pl.when(z - k >= 0)
        def _():
            feature_copy(z - k, b, fwd_sem.at[b, z - k], z).wait_recv()

            @pl.when(z < n_g - 1)
            def _():
                feature_copy(z - k, b, fwd_sem.at[b, z - k], z + 1).start()

        @pl.when(z + k < n_g)
        def _():
            feature_copy(z + k, b, fwd_sem.at[b, z + k], z).wait_recv()

            @pl.when(z > 0)
            def _():
                feature_copy(z + k, b, fwd_sem.at[b, z + k], z - 1).start()

    def gather(b):
        @pl.when(b + AHEAD < nb)
        def _():
            own_start(b + AHEAD)

        @pl.when(b + NEAR < nb)
        def _():
            take(b + NEAR, 1)

        for k in range(2, n_g):
            take(b, k)

    cuts = block_len // blk

    def own_block(b):
        for at in range(b * cuts, (b + 1) * cuts):
            if at < AHEAD:
                own_start(at)
            else:
                @pl.when(jnp.logical_not(inner))
                def _():
                    own_start(at)

    own_block(0)
    for phase in range(n_bits):
        weight_own(phase)
    for b in range(1, n_blocks):
        pick(b)
        own_block(b)
    copies_in[2].wait()
    live = lax.broadcasted_iota(jnp.int32, (n_blocks, block_len), 0) < count[0]
    weights = jnp.where(live, route[...], 0.0)
    for b in range(n_blocks):
        turned = jnp.broadcast_to(weights[b : b + 1, :], (block_len, block_len)).T
        coef[b * block_len : (b + 1) * block_len, :] = turned
    for copy in copies_in[3:]:
        copy.wait()

    groups = [(phase, group) for phase in range(n_bits) for group in range(phase + 1)]

    @pl.when(inner)
    def _():
        for b in range(NEAR):
            take(b, 1)

    early = [pair for pair in groups if pair[0] < n_bits - 1]
    for at, (phase, group) in enumerate(early):
        weight_pass(phase, group)
        for b in range(at * LEAD // len(early), (at + 1) * LEAD // len(early)):
            @pl.when(inner)
            def _():
                gather(b)

    for phase, group in groups[len(early) :]:
        weight_pass(phase, group)

    def block_step(b):
        span = pl.ds(pl.multiple_of(b * blk, blk), blk)
        gate = jnp.zeros((blk, width), F32)
        up = jnp.zeros((blk, width), F32)
        for s in range(n_g):
            x = routed[s, span, :]
            gate += jnp.dot(x, wg[s * fw : (s + 1) * fw, :], preferred_element_type=F32)
            up += jnp.dot(x, wu[s * fw : (s + 1) * fw, :], preferred_element_type=F32)
        c = jnp.concatenate([coef[span, :]] * (width // coef.shape[1]), axis=1)
        sig = jax.nn.sigmoid(gate)
        act = gate * sig
        hidden[span, :] = (c * act * up).astype(BF16)
        scaled = grad_hidden[span, :].astype(F32) * c
        gg = (scaled * up * sig * (1.0 + gate * (1.0 - sig))).astype(BF16)
        gu = (scaled * act).astype(BF16)
        grads[span, :width] = gg
        grads[span, width:] = gu
        for d in range(n_g):
            back = lax.dot_general(
                gg, wg[d * fw : (d + 1) * fw, :], BACK, preferred_element_type=F32
            )
            back += lax.dot_general(
                gu, wu[d * fw : (d + 1) * fw, :], BACK, preferred_element_type=F32
            )
            part[b, d] = back

    def row_copy(b, d, right):
        return pltpu.make_async_remote_copy(
            src_ref=outgoing.at[b, d],
            dst_ref=(from_left if right else from_right).at[b, d],
            send_sem=rs_send.at[b, d],
            recv_sem=(left_sem if right else right_sem).at[b, d],
            device_id={"group": z + 1 if right else z - 1},
        )

    def end_send(b, d, right):
        outgoing[b, d] = part[b, d].astype(BF16)
        row_copy(b, d, right).start()

    def flow_far(b):
        @pl.when(z == 0)
        def _():
            for d in range(n_g - 1, 1, -1):
                end_send(b, d, True)

        @pl.when(z == n_g - 1)
        def _():
            for d in range(n_g - 2):
                end_send(b, d, False)

    def flow_near(b):
        @pl.when(z == 0)
        def _():
            end_send(b, 1, True)

        @pl.when(z == n_g - 1)
        def _():
            end_send(b, n_g - 2, False)

    def flow_inner(s):
        right_b = s - HOP * (z - 1)

        @pl.when(inner & (right_b >= 0) & (right_b < nb))
        def _():
            for k in range(n_g - 1, 0, -1):
                d = z + k

                @pl.when(d < n_g)
                def _():
                    row_copy(right_b, d, True).wait_recv()
                    outgoing[right_b, d] = (
                        part[right_b, d] + from_left[right_b, d].astype(F32)
                    ).astype(BF16)
                    row_copy(right_b, d, True).start()

        left_b = s - HOP * (n_g - 2 - z)

        @pl.when(inner & (left_b >= 0) & (left_b < nb))
        def _():
            for k in range(n_g - 1, 0, -1):
                d = z - k

                @pl.when(d >= 0)
                def _():
                    row_copy(left_b, d, False).wait_recv()
                    outgoing[left_b, d] = (
                        part[left_b, d] + from_right[left_b, d].astype(F32)
                    ).astype(BF16)
                    row_copy(left_b, d, False).start()

    begin = nb - 1 - LEAD

    def stage(s, carry):
        @pl.when(inner & (s + LEAD < nb))
        def _():
            gather(s + LEAD)

        @pl.when(jnp.logical_not(inner))
        def _():
            for k in range(1, n_g):
                take(s, k)

        block_step(s)
        flow_far(s)

        @pl.when(s >= DEFER)
        def _():
            flow_near(s - DEFER)

        @pl.when(s >= begin)
        def _():
            flow_inner(s - begin)

        return carry

    lax.fori_loop(0, nb, stage, 0)
    for b in range(nb - DEFER, nb):
        flow_near(b)

    totals = ((sum_g, stage_g, got_g), (sum_u, stage_u, got_u))
    paths = [order[::-1] for order in orders]
    small = w_rows % 128 > 0

    def weight_grad(which, owner):
        total = totals[which][0]
        chunk = pl.ds(pl.multiple_of(owner * w_rows, w_rows), w_rows)
        if small:
            return total[chunk, :]
        per = fw // w_rows
        across = pl.ds(pl.multiple_of((owner % per) * w_rows, w_rows), w_rows)
        return lax.dot_general(
            routed[owner // per, :, across],
            grads[:, which * width : (which + 1) * width],
            BOTH,
            preferred_element_type=F32,
        )

    def half_count(phase):
        return 2 ** max(n_bits - 2 - phase, 0)

    def half_sides(phase):
        return range(2 if phase < n_bits - 1 else 1)

    def half_at(phase, side, i):
        start = sum(2 ** (n_bits - 1 - t) for t in range(phase))
        at = (start + side * half_count(phase) + i) * w_rows
        return slice(at, at + w_rows)

    def half_owner(which, phase, side, i, mine):
        path = paths[which]
        bits = [] if mine else [path[phase]]
        if phase < n_bits - 1 and side == 0:
            bits.append(path[phase + 1])
        bits += [k for at, k in enumerate(path[phase + 2 :]) if (i >> at) & 1]
        return flipped(bits)

    def half_copy(which, phase, side):
        total, stage_ref, got = totals[which]
        at = half_at(phase, side, 0).start
        span = pl.ds(at, half_count(phase) * w_rows)
        return pltpu.make_async_remote_copy(
            src_ref=stage_ref.at[span],
            dst_ref=got.at[span],
            send_sem=h_send.at[which, phase, side],
            recv_sem=h_recv.at[which, phase, side],
            device_id={"dp": partner(paths[which][phase])},
        )

    def half_begin():
        if small:
            for s in range(n_g):
                made = lax.dot_general(
                    routed[s], grads[...], BOTH, preferred_element_type=F32
                )
                sum_g[s * fw : (s + 1) * fw, :] = made[:, :width]
                sum_u[s * fw : (s + 1) * fw, :] = made[:, width:]
        for side in half_sides(0):
            for which in range(2):
                for i in range(half_count(0)):
                    made = weight_grad(which, half_owner(which, 0, side, i, False))
                    totals[which][1][half_at(0, side, i), :] = made.astype(BF16)
                half_copy(which, 0, side).start()
        if not small:
            for side in half_sides(0):
                for which in range(2):
                    for i in range(half_count(0)):
                        owner = half_owner(which, 0, side, i, True)
                        chunk = pl.ds(pl.multiple_of(owner * w_rows, w_rows), w_rows)
                        totals[which][0][chunk, :] = weight_grad(which, owner)

    def half_pass(phase, side):
        for which in range(2):
            total, stage_ref, got = totals[which]
            half_copy(which, phase, side).wait_recv()
            for i in range(half_count(phase)):
                owner = half_owner(which, phase, side, i, True)
                chunk = pl.ds(pl.multiple_of(owner * w_rows, w_rows), w_rows)
                value = total[chunk, :] + got[half_at(phase, side, i), :].astype(F32)
                if phase == n_bits - 1:
                    (grad_gate_w, grad_up_w)[which][...] = value * factor
                elif side == 1:
                    total[chunk, :] = value
                elif phase == n_bits - 2:
                    stage_ref[half_at(phase + 1, 0, 0), :] = value.astype(BF16)
                else:
                    at = half_at(phase + 1, 1 - i % 2, i // 2)
                    stage_ref[at, :] = value.astype(BF16)
            if phase < n_bits - 1 and side == 0:
                for later in half_sides(phase + 1):
                    half_copy(which, phase + 1, later).start()

    half_begin()
    steps = list(range(nb - begin, nb + HOP * (n_g - 3)))
    for phase in range(n_bits):
        for step in steps[phase : phase + 1]:
            flow_inner(step)
        for side in half_sides(phase):
            half_pass(phase, side)
    for step in steps[n_bits:]:
        flow_inner(step)

    for b in range(nb):
        @pl.when(z > 0)
        def _():
            row_copy(b, z, True).wait_recv()

        @pl.when(z < n_g - 1)
        def _():
            row_copy(b, z, False).wait_recv()

        span = slice(b * blk, (b + 1) * blk)

        @pl.when(z == 0)
        def _():
            landed[span, :] = (part[b, z] + from_right[b, z].astype(F32)).astype(BF16)

        @pl.when(z == n_g - 1)
        def _():
            landed[span, :] = (part[b, z] + from_left[b, z].astype(F32)).astype(BF16)

        @pl.when(inner)
        def _():
            landed[span, :] = (
                part[b, z] + from_left[b, z].astype(F32) + from_right[b, z].astype(F32)
            ).astype(BF16)

    tile = min(n_tok, 256)

    def place(t, carry):
        at = pl.ds(pl.multiple_of(t * tile, tile), tile)
        grad_tokens[at, :] = jnp.dot(
            onehot[at, :], landed[...], preferred_element_type=F32
        ).astype(BF16)
        return carry

    lax.fori_loop(0, n_tok // tile, place, 0)

    def drain(b, carry):
        @pl.when(z > 0)
        def _():
            own_left(b).wait_send()

        @pl.when(z < n_g - 1)
        def _():
            own_right(b).wait_send()

        for s in range(n_g):
            @pl.when(((s < z) & (z < n_g - 1)) | ((s > z) & (z > 0)))
            def _():
                feature_copy(s, b, fwd_sem.at[b, s], z).wait_send()

            @pl.when(s > z)
            def _():
                row_copy(b, s, True).wait_send()

            @pl.when(s < z)
            def _():
                row_copy(b, s, False).wait_send()

        return carry

    lax.fori_loop(0, nb, drain, 0)
    for which in range(2):
        for phase, group in groups:
            weight_whole(which, phase, group).wait_send()
        for phase in range(n_bits):
            for side in half_sides(phase):
                half_copy(which, phase, side).wait_send()


def store(*refs):
    sems = refs[-1]
    half = (len(refs) - 1) // 2
    copies = [
        pltpu.make_async_copy(refs[i], refs[half + i], sems.at[i]) for i in range(half)
    ]
    for copy in copies:
        copy.start()
    for copy in copies:
        copy.wait()


def shards(n_dp, n_g, tokens, gate_w, up_w, block_rows, block_count, route_gate, grad_hidden):
    n_blocks, block_len = block_rows.shape
    nb, blk = n_blocks * CUTS, block_len // CUTS
    n_tok, fw = tokens.shape
    w_rows, width = gate_w.shape
    routed_len = nb * blk
    depth = n_dp * w_rows
    n_bits = n_dp.bit_length() - 1
    factor = float((n_dp * routed_len) ** (-0.5))
    dma = pltpu.SemaphoreType.DMA
    vmem = pl.BlockSpec(memory_space=pltpu.VMEM)
    hbm = pl.BlockSpec(memory_space=pltpu.HBM)
    smem = pl.BlockSpec(memory_space=pltpu.SMEM)
    kept = routed_len * width * 2 + n_tok * fw * 2 + 2 * w_rows * width * 4
    made = pl.pallas_call(
        functools.partial(kernel, n_dp, n_g, factor),
        out_shape=(
            pltpu.VMEM((routed_len, width), BF16),
            pltpu.VMEM((n_tok, fw), BF16),
            pltpu.VMEM((w_rows, width), F32),
            pltpu.VMEM((w_rows, width), F32),
        ),
        in_specs=[hbm, hbm, hbm, hbm, smem, hbm, hbm],
        out_specs=(vmem, vmem, vmem, vmem),
        scratch_shapes=[
            pltpu.VMEM((n_tok, fw), BF16),
            pltpu.VMEM((n_blocks, block_len), jnp.int32),
            pltpu.VMEM((n_blocks, block_len), F32),
            pltpu.VMEM((routed_len, width), BF16),
            pltpu.VMEM((n_tok, routed_len), BF16),
            pltpu.VMEM((routed_len, block_len), F32),
            pltpu.VMEM((n_g, routed_len, fw), BF16),
            pltpu.VMEM((depth, width), BF16),
            pltpu.VMEM((depth, width), BF16),
            pltpu.VMEM((routed_len, 2 * width), BF16),
            pltpu.VMEM((nb, n_g, blk, fw), F32),
            pltpu.VMEM((nb, n_g, blk, fw), BF16),
            pltpu.VMEM((nb, n_g, blk, fw), BF16),
            pltpu.VMEM((nb, n_g, blk, fw), BF16),
            pltpu.VMEM((routed_len, fw), BF16),
            pltpu.VMEM((depth, width), F32),
            pltpu.VMEM((depth, width), F32),
            pltpu.VMEM((depth, width), BF16),
            pltpu.VMEM((depth, width), BF16),
            pltpu.VMEM((depth, width), BF16),
            pltpu.VMEM((depth, width), BF16),
            dma((nb, 2)),
            dma((nb, n_g)),
            dma((nb, n_g)),
            dma((2, n_bits, n_bits)),
            dma((2, n_bits, n_bits)),
            dma((nb, n_g)),
            dma((nb, n_g)),
            dma((nb, n_g)),
            dma((2, n_bits, 2)),
            dma((2, n_bits, 2)),
            dma((6,)),
        ],
        compiler_params=pltpu.CompilerParams(
            collective_id=0, has_side_effects=True, vmem_limit_bytes=67043328 - kept
        ),
    )(tokens, gate_w, up_w, block_rows, block_count, route_gate, grad_hidden)
    return pl.pallas_call(
        store,
        out_shape=tuple(jax.ShapeDtypeStruct(x.shape, x.dtype) for x in made),
        in_specs=[vmem] * len(made),
        out_specs=(hbm,) * len(made),
        scratch_shapes=[dma((len(made),))],
        compiler_params=pltpu.CompilerParams(vmem_limit_bytes=2**20),
    )(*made)


def solution(mesh):
    return jax.shard_map(
        functools.partial(shards, mesh.shape["dp"], mesh.shape["group"]),
        mesh=mesh,
        in_specs=(
            P("dp", "group"),
            P("dp", "group"),
            P("dp", "group"),
            P("dp", None),
            P("dp"),
            P("dp", None),
            P("dp", "group"),
        ),
        out_specs=(P("dp", "group"), P("dp", "group"), P("dp", "group"), P("dp", "group")),
        check_vma=False,
    )
```

```python
import functools

import jax
import jax.numpy as jnp
from jax import lax
from jax.experimental import pallas as pl
from jax.experimental.pallas import tpu as pltpu
from jax.sharding import PartitionSpec as P

F32 = jnp.float32
BF16 = jnp.bfloat16
CUTS = 2
AHEAD = 4
NEAR = 2
LEAD = 2
HOP = 2
LATE = 4
LAST = 2
EARLY = 0
BOTH = (((0,), (0,)), ((), ()))
BACK = (((1,), (1,)), ((), ()))


def kernel(
    n_dp,
    n_g,
    factor,
    tokens_in,
    gate_w,
    up_w,
    rows_in,
    count,
    route_in,
    grad_in,
    hidden,
    grad_tokens,
    grad_gate_w,
    grad_up_w,
    tokens,
    rows,
    route,
    grad_hidden,
    onehot,
    coef,
    routed,
    wg,
    wu,
    grads,
    part,
    outgoing,
    from_left,
    from_right,
    landed,
    sum_g,
    sum_u,
    stage_g,
    stage_u,
    got_g,
    got_u,
    own_sem,
    fwd_sem,
    ag_sem,
    w_send,
    w_recv,
    rs_send,
    left_sem,
    right_sem,
    h_send,
    h_recv,
    local_sem,
):
    n_blocks, block_len = rows.shape
    nb, blk = part.shape[0], part.shape[2]
    n_tok, fw = tokens.shape
    w_rows, width = gate_w.shape
    n_bits = n_dp.bit_length() - 1
    p = lax.axis_index("dp")
    z = lax.axis_index("group")

    def bit(k):
        return (p // 2**k) % 2

    def partner(k):
        return p + 2**k - bit(k) * 2 ** (k + 1)

    upper = list(range(1, n_bits))
    orders = (upper + [0], upper[::-1] + [0])
    inner = (z > 0) & (z < n_g - 1)

    def flipped(bits):
        return p + sum((1 - 2 * bit(k)) * 2**k for k in bits)

    copies_in = [
        pltpu.make_async_copy(source, dest, local_sem.at[i])
        for i, (source, dest) in enumerate(
            (
                (tokens_in, tokens),
                (rows_in, rows),
                (route_in, route),
                (gate_w, wg.at[pl.ds(p * w_rows, w_rows)]),
                (up_w, wu.at[pl.ds(p * w_rows, w_rows)]),
                (grad_in, grad_hidden),
            )
        )
    ]
    for copy in copies_in:
        copy.start()

    barrier = pltpu.get_barrier_semaphore()
    for k in range(n_bits):
        pl.semaphore_signal(barrier, inc=1, device_id={"dp": partner(k)})

    @pl.when(z > 0)
    def _():
        pl.semaphore_signal(barrier, inc=1, device_id={"group": z - 1})

    @pl.when(z < n_g - 1)
    def _():
        pl.semaphore_signal(barrier, inc=1, device_id={"group": z + 1})

    def pick(b):
        span = slice(b * block_len, (b + 1) * block_len)
        hot = lax.broadcasted_iota(jnp.int32, (n_tok, block_len), 0) == rows[b : b + 1, :]
        hot = jnp.where(hot, 1.0, 0.0).astype(BF16)
        onehot[:, span] = hot
        picked = lax.dot_general(hot, tokens[...], BOTH, preferred_element_type=F32)
        routed[z, span, :] = picked.astype(BF16)

    copies_in[0].wait()
    copies_in[1].wait()
    pick(0)
    sides = jnp.minimum(z, 1) + jnp.minimum(n_g - 1 - z, 1)
    pl.semaphore_wait(barrier, n_bits + sides)

    def weight_copy(which, phase, group, owner):
        source, dest = ((gate_w, wg), (up_w, wu))[which]
        place = dest.at[pl.ds(pl.multiple_of(owner * w_rows, w_rows), w_rows)]
        return pltpu.make_async_remote_copy(
            src_ref=place if group else source,
            dst_ref=place,
            send_sem=w_send.at[which, phase, group],
            recv_sem=w_recv.at[which, phase, group],
            device_id={"dp": partner(orders[which][phase])},
        )

    def weight_whole(which, phase, group):
        span = (wg, wu)[which].at[pl.ds(0, w_rows * (2 ** (group - 1) if group else 1))]
        return pltpu.make_async_remote_copy(
            src_ref=span,
            dst_ref=span,
            send_sem=w_send.at[which, phase, group],
            recv_sem=w_recv.at[which, phase, group],
            device_id={"dp": partner(orders[which][phase])},
        )

    def weight_own(phase):
        for which in range(2):
            weight_copy(which, phase, 0, p).start()

    def weight_pass(phase, group):
        for which in range(2):
            order = orders[which]
            weight_whole(which, phase, group).wait_recv()
            low = order[: group - 1] if group else []
            for later in range(phase + 1, n_bits):
                for number in range(2 ** len(low)):
                    bits = [order[phase]] + ([order[group - 1]] if group else [])
                    bits += [k for at, k in enumerate(low) if (number >> at) & 1]
                    weight_copy(which, later, phase + 1, flipped(bits)).start()

    def feature_copy(s, b, send_sem, to):
        place = routed.at[s, pl.ds(pl.multiple_of(b * blk, blk), blk)]
        return pltpu.make_async_remote_copy(
            src_ref=place,
            dst_ref=place,
            send_sem=send_sem,
            recv_sem=ag_sem.at[b, s],
            device_id={"group": to},
        )

    def own_left(b):
        return feature_copy(z, b, own_sem.at[b, 0], z - 1)

    def own_right(b):
        return feature_copy(z, b, own_sem.at[b, 1], z + 1)

    def own_start(b):
        @pl.when(z > 0)
        def _():
            own_left(b).start()

        @pl.when(z < n_g - 1)
        def _():
            own_right(b).start()

    def take(b, k):
        @pl.when(z - k >= 0)
        def _():
            feature_copy(z - k, b, fwd_sem.at[b, z - k], z).wait_recv()

            @pl.when(z < n_g - 1)
            def _():
                feature_copy(z - k, b, fwd_sem.at[b, z - k], z + 1).start()

        @pl.when(z + k < n_g)
        def _():
            feature_copy(z + k, b, fwd_sem.at[b, z + k], z).wait_recv()

            @pl.when(z > 0)
            def _():
                feature_copy(z + k, b, fwd_sem.at[b, z + k], z - 1).start()

    def gather(b):
        @pl.when(b + AHEAD < nb)
        def _():
            own_start(b + AHEAD)

        @pl.when(b + NEAR < nb)
        def _():
            take(b + NEAR, 1)

        for k in range(2, n_g):
            take(b, k)

    cuts = block_len // blk

    def own_block(b):
        for at in range(b * cuts, (b + 1) * cuts):
            if at < AHEAD:
                own_start(at)
            else:
                @pl.when(jnp.logical_not(inner))
                def _():
                    own_start(at)

    own_block(0)
    for phase in range(n_bits):
        weight_own(phase)
    for b in range(1, n_blocks):
        pick(b)
        own_block(b)
    copies_in[2].wait()
    live = lax.broadcasted_iota(jnp.int32, (n_blocks, block_len), 0) < count[0]
    weights = jnp.where(live, route[...], 0.0)
    for b in range(n_blocks):
        turned = jnp.broadcast_to(weights[b : b + 1, :], (block_len, block_len)).T
        coef[b * block_len : (b + 1) * block_len, :] = turned
    for copy in copies_in[3:]:
        copy.wait()

    groups = [(phase, group) for phase in range(n_bits) for group in range(phase + 1)]

    @pl.when(inner)
    def _():
        for b in range(NEAR):
            take(b, 1)

    early = [pair for pair in groups if pair[0] < n_bits - 1]
    for at, (phase, group) in enumerate(early):
        weight_pass(phase, group)
        for b in range(at * LEAD // len(early), (at + 1) * LEAD // len(early)):
            @pl.when(inner)
            def _():
                gather(b)

    for phase, group in groups[len(early) :]:
        weight_pass(phase, group)

    def block_step(b):
        span = pl.ds(pl.multiple_of(b * blk, blk), blk)
        gate = jnp.zeros((blk, width), F32)
        up = jnp.zeros((blk, width), F32)
        for s in range(n_g):
            x = routed[s, span, :]
            gate += jnp.dot(x, wg[s * fw : (s + 1) * fw, :], preferred_element_type=F32)
            up += jnp.dot(x, wu[s * fw : (s + 1) * fw, :], preferred_element_type=F32)
        c = jnp.concatenate([coef[span, :]] * (width // coef.shape[1]), axis=1)
        sig = jax.nn.sigmoid(gate)
        act = gate * sig
        hidden[span, :] = (c * act * up).astype(BF16)
        scaled = grad_hidden[span, :].astype(F32) * c
        gg = (scaled * up * sig * (1.0 + gate * (1.0 - sig))).astype(BF16)
        gu = (scaled * act).astype(BF16)
        grads[span, :width] = gg
        grads[span, width:] = gu
        for d in range(n_g):
            back = lax.dot_general(
                gg, wg[d * fw : (d + 1) * fw, :], BACK, preferred_element_type=F32
            )
            back += lax.dot_general(
                gu, wu[d * fw : (d + 1) * fw, :], BACK, preferred_element_type=F32
            )
            part[b, d] = back

    def row_copy(b, d, right):
        return pltpu.make_async_remote_copy(
            src_ref=outgoing.at[b, d],
            dst_ref=(from_left if right else from_right).at[b, d],
            send_sem=rs_send.at[b, d],
            recv_sem=(left_sem if right else right_sem).at[b, d],
            device_id={"group": z + 1 if right else z - 1},
        )

    def end_send(b, d, right):
        outgoing[b, d] = part[b, d].astype(BF16)
        row_copy(b, d, right).start()

    def flow_far(b):
        @pl.when(z == 0)
        def _():
            for d in range(n_g - 1, 1, -1):
                end_send(b, d, True)

        @pl.when(z == n_g - 1)
        def _():
            for d in range(n_g - 2):
                end_send(b, d, False)

    def flow_near(b):
        @pl.when(z == 0)
        def _():
            end_send(b, 1, True)

        @pl.when(z == n_g - 1)
        def _():
            end_send(b, n_g - 2, False)

    def relay(b, d, right):
        row_copy(b, d, right).wait_recv()
        come = (from_left if right else from_right)[b, d]
        outgoing[b, d] = (part[b, d] + come.astype(F32)).astype(BF16)
        row_copy(b, d, right).start()

    def flow_side(b, right):
        final = n_g - 1 if right else 0

        @pl.when(inner & (b >= 0) & (b < nb))
        def _():
            for k in range(n_g - 1, 0, -1):
                d = z + k if right else z - k
                go = (d < n_g) if right else (d >= 0)
                if k == 1:
                    go = go & ((d == final) | (b < nb - LAST))

                @pl.when(go)
                def _():
                    relay(b, d, right)

        d = z + 1 if right else z - 1

        @pl.when(inner & (b == nb - 1) & (d != final))
        def _():
            for late in range(nb - LAST, nb):
                relay(late, d, right)

    def flow_inner(s):
        flow_side(s - HOP * (z - 1), True)
        flow_side(s - HOP * (n_g - 2 - z), False)

    begin = nb - 1 - LEAD - EARLY

    def stage(s, carry):
        @pl.when(inner & (s + LEAD < nb))
        def _():
            gather(s + LEAD)

        @pl.when(jnp.logical_not(inner))
        def _():
            for k in range(1, n_g):
                take(s, k)

        @pl.when(s >= begin)
        def _():
            flow_inner(s - begin)

        block_step(s)
        flow_far(s)

        @pl.when(s < nb - LATE)
        def _():
            flow_near(s)

        return carry

    lax.fori_loop(0, nb, stage, 0)
    for b in range(nb - LATE, nb):
        flow_near(b)

    totals = ((sum_g, stage_g, got_g), (sum_u, stage_u, got_u))
    paths = [order[::-1] for order in orders]
    small = w_rows % 128 > 0

    def weight_grad(which, owner):
        total = totals[which][0]
        chunk = pl.ds(pl.multiple_of(owner * w_rows, w_rows), w_rows)
        if small:
            return total[chunk, :]
        per = fw // w_rows
        across = pl.ds(pl.multiple_of((owner % per) * w_rows, w_rows), w_rows)
        return lax.dot_general(
            routed[owner // per, :, across],
            grads[:, which * width : (which + 1) * width],
            BOTH,
            preferred_element_type=F32,
        )

    def half_groups(phase):
        if phase < n_bits - 2:
            return [(0, 1), (0, 0), (1, 1), (1, 0)]
        return [(0, 0), (1, 0)] if phase == n_bits - 2 else [(0, 0)]

    def half_count(phase):
        return 2 ** max(n_bits - 3 - phase, 0)

    def half_at(phase, group, i):
        start = sum(2 ** (n_bits - 1 - t) for t in range(phase))
        at = start + half_groups(phase).index(group) * half_count(phase) + i
        return slice(at * w_rows, (at + 1) * w_rows)

    def half_owner(which, phase, group, i, mine):
        path = paths[which]
        bits = [] if mine else [path[phase]]
        if phase < n_bits - 1 and group[0] == 0:
            bits.append(path[phase + 1])
        if phase < n_bits - 2 and group[1] == 1:
            bits.append(path[phase + 2])
        bits += [k for at, k in enumerate(path[phase + 3 :]) if (i >> at) & 1]
        return flipped(bits)

    def half_copy(which, phase, group):
        total, stage_ref, got = totals[which]
        at = half_at(phase, group, 0).start
        span = pl.ds(at, half_count(phase) * w_rows)
        number = half_groups(phase).index(group)
        return pltpu.make_async_remote_copy(
            src_ref=stage_ref.at[span],
            dst_ref=got.at[span],
            send_sem=h_send.at[which, phase, number],
            recv_sem=h_recv.at[which, phase, number],
            device_id={"dp": partner(paths[which][phase])},
        )

    def half_first(group):
        for which in range(2):
            for i in range(half_count(0)):
                made = weight_grad(which, half_owner(which, 0, group, i, False))
                totals[which][1][half_at(0, group, i), :] = made.astype(BF16)
            half_copy(which, 0, group).start()

    def half_keep(group):
        for which in range(2):
            for i in range(half_count(0)):
                owner = half_owner(which, 0, group, i, True)
                chunk = pl.ds(pl.multiple_of(owner * w_rows, w_rows), w_rows)
                totals[which][0][chunk, :] = weight_grad(which, owner)

    def half_begin():
        if small:
            for s in range(n_g):
                made = lax.dot_general(
                    routed[s], grads[...], BOTH, preferred_element_type=F32
                )
                sum_g[s * fw : (s + 1) * fw, :] = made[:, :width]
                sum_u[s * fw : (s + 1) * fw, :] = made[:, width:]
        todo = half_groups(0)
        half = max(len(todo) // 2, 1)
        for group in todo[:half]:
            half_first(group)
        for group in todo[: 0 if small else half]:
            half_keep(group)
        for group in todo[half:]:
            half_first(group)
        for group in todo[0 if small else half : 0 if small else len(todo)]:
            half_keep(group)

    def half_pass(phase, group):
        side, sub = group
        after = 1 - sub if phase < n_bits - 2 else 0
        for which in range(2):
            total, stage_ref, got = totals[which]
            half_copy(which, phase, group).wait_recv()
            for i in range(half_count(phase)):
                owner = half_owner(which, phase, group, i, True)
                chunk = pl.ds(pl.multiple_of(owner * w_rows, w_rows), w_rows)
                value = total[chunk, :] + got[half_at(phase, group, i), :].astype(F32)
                if phase == n_bits - 1:
                    (grad_gate_w, grad_up_w)[which][...] = value * factor
                elif side == 1:
                    total[chunk, :] = value
                elif phase + 1 < n_bits - 2:
                    at = half_at(phase + 1, (after, i % 2), i // 2)
                    stage_ref[at, :] = value.astype(BF16)
                else:
                    stage_ref[half_at(phase + 1, (after, 0), 0), :] = value.astype(BF16)
            if phase < n_bits - 1 and side == 0:
                for later in half_groups(phase + 1):
                    if phase == n_bits - 2 or later[0] == after:
                        half_copy(which, phase + 1, later).start()

    half_begin()
    steps = list(range(nb - begin, nb + HOP * (n_g - 3)))
    for phase in range(n_bits):
        for step in steps[phase : phase + 1]:
            flow_inner(step)
        for group in half_groups(phase):
            half_pass(phase, group)
    for step in steps[n_bits:]:
        flow_inner(step)

    for b in range(nb):
        @pl.when(z > 0)
        def _():
            row_copy(b, z, True).wait_recv()

        @pl.when(z < n_g - 1)
        def _():
            row_copy(b, z, False).wait_recv()

        span = slice(b * blk, (b + 1) * blk)

        @pl.when(z == 0)
        def _():
            landed[span, :] = (part[b, z] + from_right[b, z].astype(F32)).astype(BF16)

        @pl.when(z == n_g - 1)
        def _():
            landed[span, :] = (part[b, z] + from_left[b, z].astype(F32)).astype(BF16)

        @pl.when(inner)
        def _():
            landed[span, :] = (
                part[b, z] + from_left[b, z].astype(F32) + from_right[b, z].astype(F32)
            ).astype(BF16)

    tile = min(n_tok, 256)

    def place(t, carry):
        at = pl.ds(pl.multiple_of(t * tile, tile), tile)
        grad_tokens[at, :] = jnp.dot(
            onehot[at, :], landed[...], preferred_element_type=F32
        ).astype(BF16)
        return carry

    lax.fori_loop(0, n_tok // tile, place, 0)

    def drain(b, carry):
        @pl.when(z > 0)
        def _():
            own_left(b).wait_send()

        @pl.when(z < n_g - 1)
        def _():
            own_right(b).wait_send()

        for s in range(n_g):
            @pl.when(((s < z) & (z < n_g - 1)) | ((s > z) & (z > 0)))
            def _():
                feature_copy(s, b, fwd_sem.at[b, s], z).wait_send()

            @pl.when(s > z)
            def _():
                row_copy(b, s, True).wait_send()

            @pl.when(s < z)
            def _():
                row_copy(b, s, False).wait_send()

        return carry

    lax.fori_loop(0, nb, drain, 0)
    for which in range(2):
        for phase, group in groups:
            weight_whole(which, phase, group).wait_send()
        for phase in range(n_bits):
            for group in half_groups(phase):
                half_copy(which, phase, group).wait_send()


def store(*refs):
    sems = refs[-1]
    half = (len(refs) - 1) // 2
    copies = [
        pltpu.make_async_copy(refs[i], refs[half + i], sems.at[i]) for i in range(half)
    ]
    for copy in copies:
        copy.start()
    for copy in copies:
        copy.wait()


def shards(n_dp, n_g, tokens, gate_w, up_w, block_rows, block_count, route_gate, grad_hidden):
    n_blocks, block_len = block_rows.shape
    nb, blk = n_blocks * CUTS, block_len // CUTS
    n_tok, fw = tokens.shape
    w_rows, width = gate_w.shape
    routed_len = nb * blk
    depth = n_dp * w_rows
    n_bits = n_dp.bit_length() - 1
    factor = float((n_dp * routed_len) ** (-0.5))
    dma = pltpu.SemaphoreType.DMA
    vmem = pl.BlockSpec(memory_space=pltpu.VMEM)
    hbm = pl.BlockSpec(memory_space=pltpu.HBM)
    smem = pl.BlockSpec(memory_space=pltpu.SMEM)
    kept = routed_len * width * 2 + n_tok * fw * 2 + 2 * w_rows * width * 4
    made = pl.pallas_call(
        functools.partial(kernel, n_dp, n_g, factor),
        out_shape=(
            pltpu.VMEM((routed_len, width), BF16),
            pltpu.VMEM((n_tok, fw), BF16),
            pltpu.VMEM((w_rows, width), F32),
            pltpu.VMEM((w_rows, width), F32),
        ),
        in_specs=[hbm, hbm, hbm, hbm, smem, hbm, hbm],
        out_specs=(vmem, vmem, vmem, vmem),
        scratch_shapes=[
            pltpu.VMEM((n_tok, fw), BF16),
            pltpu.VMEM((n_blocks, block_len), jnp.int32),
            pltpu.VMEM((n_blocks, block_len), F32),
            pltpu.VMEM((routed_len, width), BF16),
            pltpu.VMEM((n_tok, routed_len), BF16),
            pltpu.VMEM((routed_len, block_len), F32),
            pltpu.VMEM((n_g, routed_len, fw), BF16),
            pltpu.VMEM((depth, width), BF16),
            pltpu.VMEM((depth, width), BF16),
            pltpu.VMEM((routed_len, 2 * width), BF16),
            pltpu.VMEM((nb, n_g, blk, fw), F32),
            pltpu.VMEM((nb, n_g, blk, fw), BF16),
            pltpu.VMEM((nb, n_g, blk, fw), BF16),
            pltpu.VMEM((nb, n_g, blk, fw), BF16),
            pltpu.VMEM((routed_len, fw), BF16),
            pltpu.VMEM((depth, width), F32),
            pltpu.VMEM((depth, width), F32),
            pltpu.VMEM((depth, width), BF16),
            pltpu.VMEM((depth, width), BF16),
            pltpu.VMEM((depth, width), BF16),
            pltpu.VMEM((depth, width), BF16),
            dma((nb, 2)),
            dma((nb, n_g)),
            dma((nb, n_g)),
            dma((2, n_bits, n_bits)),
            dma((2, n_bits, n_bits)),
            dma((nb, n_g)),
            dma((nb, n_g)),
            dma((nb, n_g)),
            dma((2, n_bits, 4)),
            dma((2, n_bits, 4)),
            dma((6,)),
        ],
        compiler_params=pltpu.CompilerParams(
            collective_id=0, has_side_effects=True, vmem_limit_bytes=67043328 - kept
        ),
    )(tokens, gate_w, up_w, block_rows, block_count, route_gate, grad_hidden)
    return pl.pallas_call(
        store,
        out_shape=tuple(jax.ShapeDtypeStruct(x.shape, x.dtype) for x in made),
        in_specs=[vmem] * len(made),
        out_specs=(hbm,) * len(made),
        scratch_shapes=[dma((len(made),))],
        compiler_params=pltpu.CompilerParams(vmem_limit_bytes=2**20),
    )(*made)


def solution(mesh):
    return jax.shard_map(
        functools.partial(shards, mesh.shape["dp"], mesh.shape["group"]),
        mesh=mesh,
        in_specs=(
            P("dp", "group"),
            P("dp", "group"),
            P("dp", "group"),
            P("dp", None),
            P("dp"),
            P("dp", None),
            P("dp", "group"),
        ),
        out_specs=(P("dp", "group"), P("dp", "group"), P("dp", "group"), P("dp", "group")),
        check_vma=False,
    )
```

```python
import functools

import jax
import jax.numpy as jnp
from jax import lax
from jax.experimental import pallas as pl
from jax.experimental.pallas import tpu as pltpu
from jax.sharding import PartitionSpec as P

F32 = jnp.float32
BF16 = jnp.bfloat16
CUTS = 2
AHEAD = 4
NEAR = 2
LEAD = 2
HOP = 2
LATE = 4
LAST = 2
EARLY = 0
TILES = 4
PRE = (1, 2)
GO = (1, 2, 0)
BOTH = (((0,), (0,)), ((), ()))
BACK = (((1,), (1,)), ((), ()))


def kernel(
    n_dp,
    n_g,
    factor,
    tokens_in,
    gate_w,
    up_w,
    rows_in,
    count_in,
    route_in,
    grad_in,
    hidden,
    grad_gate_w,
    grad_up_w,
    onehot,
    landed,
    tokens,
    rows,
    route,
    count,
    grad_hidden,
    coef,
    routed,
    wg,
    wu,
    grads,
    part,
    outgoing,
    from_left,
    from_right,
    sum_g,
    sum_u,
    stage_g,
    stage_u,
    got_g,
    got_u,
    own_sem,
    fwd_sem,
    ag_sem,
    w_send,
    w_recv,
    rs_send,
    left_sem,
    right_sem,
    h_send,
    h_recv,
    local_sem,
):
    n_blocks, block_len = rows.shape
    nb, blk = part.shape[0], part.shape[2]
    n_tok, fw = tokens.shape
    w_rows, width = gate_w.shape
    n_bits = n_dp.bit_length() - 1
    p = lax.axis_index("dp")
    z = lax.axis_index("group")

    def bit(k):
        return (p // 2**k) % 2

    def partner(k):
        return p + 2**k - bit(k) * 2 ** (k + 1)

    upper = list(range(1, n_bits))
    orders = (upper + [0], upper[::-1] + [0])
    inner = (z > 0) & (z < n_g - 1)

    def flipped(bits):
        return p + sum((1 - 2 * bit(k)) * 2**k for k in bits)

    copies_in = [
        pltpu.make_async_copy(source, dest, local_sem.at[i])
        for i, (source, dest) in enumerate(
            (
                (tokens_in, tokens),
                (rows_in, rows),
                (route_in, route),
                (count_in, count),
                (gate_w, wg.at[pl.ds(p * w_rows, w_rows)]),
                (up_w, wu.at[pl.ds(p * w_rows, w_rows)]),
                (grad_in, grad_hidden),
            )
        )
    ]
    for copy in copies_in:
        copy.start()

    barrier = pltpu.get_barrier_semaphore()
    for k in range(n_bits):
        pl.semaphore_signal(barrier, inc=1, device_id={"dp": partner(k)})

    @pl.when(z > 0)
    def _():
        pl.semaphore_signal(barrier, inc=1, device_id={"group": z - 1})

    @pl.when(z < n_g - 1)
    def _():
        pl.semaphore_signal(barrier, inc=1, device_id={"group": z + 1})

    def pick(b):
        span = slice(b * block_len, (b + 1) * block_len)
        hot = lax.broadcasted_iota(jnp.int32, (n_tok, block_len), 0) == rows[b : b + 1, :]
        hot = jnp.where(hot, 1.0, 0.0).astype(BF16)
        onehot[:, span] = hot
        picked = lax.dot_general(hot, tokens[...], BOTH, preferred_element_type=F32)
        routed[z, span, :] = picked.astype(BF16)

    copies_in[0].wait()
    copies_in[1].wait()
    pick(0)
    sides = jnp.minimum(z, 1) + jnp.minimum(n_g - 1 - z, 1)
    pl.semaphore_wait(barrier, n_bits + sides)

    def weight_copy(which, phase, group, owner):
        source, dest = ((gate_w, wg), (up_w, wu))[which]
        place = dest.at[pl.ds(pl.multiple_of(owner * w_rows, w_rows), w_rows)]
        return pltpu.make_async_remote_copy(
            src_ref=place if group else source,
            dst_ref=place,
            send_sem=w_send.at[which, phase, group],
            recv_sem=w_recv.at[which, phase, group],
            device_id={"dp": partner(orders[which][phase])},
        )

    def weight_whole(which, phase, group):
        span = (wg, wu)[which].at[pl.ds(0, w_rows * (2 ** (group - 1) if group else 1))]
        return pltpu.make_async_remote_copy(
            src_ref=span,
            dst_ref=span,
            send_sem=w_send.at[which, phase, group],
            recv_sem=w_recv.at[which, phase, group],
            device_id={"dp": partner(orders[which][phase])},
        )

    def weight_own(phase):
        for which in range(2):
            weight_copy(which, phase, 0, p).start()

    def weight_pass(phase, group):
        for which in range(2):
            order = orders[which]
            weight_whole(which, phase, group).wait_recv()
            low = order[: group - 1] if group else []
            for later in range(phase + 1, n_bits):
                for number in range(2 ** len(low)):
                    bits = [order[phase]] + ([order[group - 1]] if group else [])
                    bits += [k for at, k in enumerate(low) if (number >> at) & 1]
                    weight_copy(which, later, phase + 1, flipped(bits)).start()

    def feature_copy(s, b, send_sem, to):
        place = routed.at[s, pl.ds(pl.multiple_of(b * blk, blk), blk)]
        return pltpu.make_async_remote_copy(
            src_ref=place,
            dst_ref=place,
            send_sem=send_sem,
            recv_sem=ag_sem.at[b, s],
            device_id={"group": to},
        )

    def own_left(b):
        return feature_copy(z, b, own_sem.at[b, 0], z - 1)

    def own_right(b):
        return feature_copy(z, b, own_sem.at[b, 1], z + 1)

    def own_start(b):
        @pl.when(z > 0)
        def _():
            own_left(b).start()

        @pl.when(z < n_g - 1)
        def _():
            own_right(b).start()

    def take(b, k):
        @pl.when(z - k >= 0)
        def _():
            feature_copy(z - k, b, fwd_sem.at[b, z - k], z).wait_recv()

            @pl.when(z < n_g - 1)
            def _():
                feature_copy(z - k, b, fwd_sem.at[b, z - k], z + 1).start()

        @pl.when(z + k < n_g)
        def _():
            feature_copy(z + k, b, fwd_sem.at[b, z + k], z).wait_recv()

            @pl.when(z > 0)
            def _():
                feature_copy(z + k, b, fwd_sem.at[b, z + k], z - 1).start()

    def gather(b):
        def own():
            @pl.when(b + AHEAD < nb)
            def _():
                own_start(b + AHEAD)

        def near():
            @pl.when(b + NEAR < nb)
            def _():
                take(b + NEAR, 1)

        def far():
            for k in range(2, n_g):
                take(b, k)

        for which in GO:
            (own, near, far)[which]()

    cuts = block_len // blk

    def own_block(b):
        for at in range(b * cuts, (b + 1) * cuts):
            if at < AHEAD:
                own_start(at)
            else:
                @pl.when(jnp.logical_not(inner))
                def _():
                    own_start(at)

    own_block(0)
    for phase in range(n_bits):
        weight_own(phase)
    for b in range(1, n_blocks):
        pick(b)
        own_block(b)
    copies_in[2].wait()
    copies_in[3].wait()
    live = lax.broadcasted_iota(jnp.int32, (n_blocks, block_len), 0) < count[0]
    weights = jnp.where(live, route[...], 0.0)
    for b in range(n_blocks):
        turned = jnp.broadcast_to(weights[b : b + 1, :], (block_len, block_len)).T
        coef[b * block_len : (b + 1) * block_len, :] = turned
    for copy in copies_in[4:]:
        copy.wait()

    groups = [(phase, group) for phase in range(n_bits) for group in range(phase + 1)]

    @pl.when(inner)
    def _():
        for b in range(NEAR):
            take(b, 1)

    early = [pair for pair in groups if pair[0] < n_bits - 1]
    for at, (phase, group) in enumerate(early):
        weight_pass(phase, group)
        for b in range(LEAD):
            if PRE[b] == at:
                @pl.when(inner)
                def _():
                    gather(b)

    for phase, group in groups[len(early) :]:
        weight_pass(phase, group)

    def block_forward(b):
        span = pl.ds(pl.multiple_of(b * blk, blk), blk)
        gate = jnp.zeros((blk, width), F32)
        up = jnp.zeros((blk, width), F32)
        for s in range(n_g):
            x = routed[s, span, :]
            gate += jnp.dot(x, wg[s * fw : (s + 1) * fw, :], preferred_element_type=F32)
            up += jnp.dot(x, wu[s * fw : (s + 1) * fw, :], preferred_element_type=F32)
        c = jnp.concatenate([coef[span, :]] * (width // coef.shape[1]), axis=1)
        sig = jax.nn.sigmoid(gate)
        act = gate * sig
        hidden[span, :] = (c * act * up).astype(BF16)
        scaled = grad_hidden[span, :].astype(F32) * c
        gg = (scaled * up * sig * (1.0 + gate * (1.0 - sig))).astype(BF16)
        gu = (scaled * act).astype(BF16)
        grads[span, :width] = gg
        grads[span, width:] = gu
        return gg, gu

    def row_copy(b, d, right):
        return pltpu.make_async_remote_copy(
            src_ref=outgoing.at[b, d],
            dst_ref=(from_left if right else from_right).at[b, d],
            send_sem=rs_send.at[b, d],
            recv_sem=(left_sem if right else right_sem).at[b, d],
            device_id={"group": z + 1 if right else z - 1},
        )

    def end_start(b, d):
        @pl.when(z == 0)
        def _():
            row_copy(b, d, True).start()

        @pl.when(z == n_g - 1)
        def _():
            row_copy(b, d, False).start()

    def block_back(b, gg, gu):
        for k in range(n_g):
            d = jnp.where(2 * z < n_g, n_g - 1 - k, k)
            place = pl.ds(pl.multiple_of(d * fw, fw), fw)
            back = lax.dot_general(gg, wg[place, :], BACK, preferred_element_type=F32)
            back += lax.dot_general(gu, wu[place, :], BACK, preferred_element_type=F32)
            part[b, d] = back
            if k < n_g - 1:
                @pl.when(jnp.logical_not(inner))
                def _():
                    outgoing[b, d] = back.astype(BF16)

            if k < n_g - 2:
                end_start(b, d)
            elif k == n_g - 2:
                @pl.when(b < nb - LATE)
                def _():
                    end_start(b, d)

    def relay(b, d, right):
        row_copy(b, d, right).wait_recv()
        come = (from_left if right else from_right)[b, d]
        outgoing[b, d] = (part[b, d] + come.astype(F32)).astype(BF16)
        row_copy(b, d, right).start()

    def flow_side(b, right):
        final = n_g - 1 if right else 0

        @pl.when(inner & (b >= 0) & (b < nb))
        def _():
            for k in range(n_g - 1, 0, -1):
                d = z + k if right else z - k
                go = (d < n_g) if right else (d >= 0)
                if k == 1:
                    go = go & ((d == final) | (b < nb - LAST))

                @pl.when(go)
                def _():
                    relay(b, d, right)

        d = z + 1 if right else z - 1

        @pl.when(inner & (b == nb - 1) & (d != final))
        def _():
            for late in range(nb - LAST, nb):
                relay(late, d, right)

    def flow_inner(s):
        flow_side(s - HOP * (z - 1), True)
        flow_side(s - HOP * (n_g - 2 - z), False)

    begin = nb - 1 - LEAD - EARLY

    def arrive(s):
        @pl.when(inner & (s + LEAD < nb))
        def _():
            gather(s + LEAD)

        @pl.when(jnp.logical_not(inner))
        def _():
            for k in range(1, n_g):
                take(s, k)

        @pl.when(s >= begin)
        def _():
            flow_inner(s - begin)

    def stage(s, carry):
        arrive(s)
        block_back(s, *block_forward(s))
        return carry

    lax.fori_loop(0, nb - 1, stage, 0)

    totals = ((sum_g, stage_g, got_g), (sum_u, stage_u, got_u))
    paths = [order[::-1] for order in orders]
    small = w_rows % 128 > 0

    def weight_grad(which, owner):
        total = totals[which][0]
        chunk = pl.ds(pl.multiple_of(owner * w_rows, w_rows), w_rows)
        if small:
            return total[chunk, :]
        per = fw // w_rows
        across = pl.ds(pl.multiple_of((owner % per) * w_rows, w_rows), w_rows)
        return lax.dot_general(
            routed[owner // per, :, across],
            grads[:, which * width : (which + 1) * width],
            BOTH,
            preferred_element_type=F32,
        )

    def half_groups(phase):
        if phase < n_bits - 2:
            return [(0, 1), (0, 0), (1, 1), (1, 0)]
        return [(0, 0), (1, 0)] if phase == n_bits - 2 else [(0, 0)]

    def half_count(phase):
        return 2 ** max(n_bits - 3 - phase, 0)

    def half_at(phase, group, i):
        start = sum(2 ** (n_bits - 1 - t) for t in range(phase))
        at = start + half_groups(phase).index(group) * half_count(phase) + i
        return slice(at * w_rows, (at + 1) * w_rows)

    def half_owner(which, phase, group, i, mine):
        path = paths[which]
        bits = [] if mine else [path[phase]]
        if phase < n_bits - 1 and group[0] == 0:
            bits.append(path[phase + 1])
        if phase < n_bits - 2 and group[1] == 1:
            bits.append(path[phase + 2])
        bits += [k for at, k in enumerate(path[phase + 3 :]) if (i >> at) & 1]
        return flipped(bits)

    def half_copy(which, phase, group):
        total, stage_ref, got = totals[which]
        at = half_at(phase, group, 0).start
        span = pl.ds(at, half_count(phase) * w_rows)
        number = half_groups(phase).index(group)
        return pltpu.make_async_remote_copy(
            src_ref=stage_ref.at[span],
            dst_ref=got.at[span],
            send_sem=h_send.at[which, phase, number],
            recv_sem=h_recv.at[which, phase, number],
            device_id={"dp": partner(paths[which][phase])},
        )

    def half_first(group):
        for which in range(2):
            for i in range(half_count(0)):
                made = weight_grad(which, half_owner(which, 0, group, i, False))
                totals[which][1][half_at(0, group, i), :] = made.astype(BF16)
            half_copy(which, 0, group).start()

    def half_keep(group):
        for which in range(2):
            for i in range(half_count(0)):
                owner = half_owner(which, 0, group, i, True)
                chunk = pl.ds(pl.multiple_of(owner * w_rows, w_rows), w_rows)
                totals[which][0][chunk, :] = weight_grad(which, owner)

    def half_begin():
        if small:
            for s in range(n_g):
                made = lax.dot_general(
                    routed[s], grads[...], BOTH, preferred_element_type=F32
                )
                sum_g[s * fw : (s + 1) * fw, :] = made[:, :width]
                sum_u[s * fw : (s + 1) * fw, :] = made[:, width:]
        for group in todo[:half]:
            half_first(group)

    def half_rest():
        for group in todo[: 0 if small else half]:
            half_keep(group)
        for group in todo[half:]:
            half_first(group)
        for group in todo[0 if small else half : 0 if small else len(todo)]:
            half_keep(group)

    def half_pass(phase, group):
        side, sub = group
        after = 1 - sub if phase < n_bits - 2 else 0
        for which in range(2):
            total, stage_ref, got = totals[which]
            half_copy(which, phase, group).wait_recv()
            for i in range(half_count(phase)):
                owner = half_owner(which, phase, group, i, True)
                chunk = pl.ds(pl.multiple_of(owner * w_rows, w_rows), w_rows)
                value = total[chunk, :] + got[half_at(phase, group, i), :].astype(F32)
                if phase == n_bits - 1:
                    (grad_gate_w, grad_up_w)[which][...] = value * factor
                elif side == 1:
                    total[chunk, :] = value
                elif phase + 1 < n_bits - 2:
                    at = half_at(phase + 1, (after, i % 2), i // 2)
                    stage_ref[at, :] = value.astype(BF16)
                else:
                    stage_ref[half_at(phase + 1, (after, 0), 0), :] = value.astype(BF16)
            if phase < n_bits - 1 and side == 0:
                for later in half_groups(phase + 1):
                    if phase == n_bits - 2 or later[0] == after:
                        half_copy(which, phase + 1, later).start()

    todo = half_groups(0)
    half = max(len(todo) // 2, 1)
    arrive(nb - 1)
    made = block_forward(nb - 1)
    half_begin()
    block_back(nb - 1, *made)
    for b in range(nb - LATE, nb):
        end_start(b, jnp.where(z == 0, 1, n_g - 2))
    half_rest()
    steps = list(range(nb - begin, nb + HOP * (n_g - 3)))
    for phase in range(n_bits):
        for step in steps[phase : phase + 1]:
            flow_inner(step)
        for group in half_groups(phase):
            half_pass(phase, group)
    for step in steps[n_bits:]:
        flow_inner(step)

    for b in range(nb):
        @pl.when(z > 0)
        def _():
            row_copy(b, z, True).wait_recv()

        @pl.when(z < n_g - 1)
        def _():
            row_copy(b, z, False).wait_recv()

        span = slice(b * blk, (b + 1) * blk)

        @pl.when(z == 0)
        def _():
            landed[span, :] = (part[b, z] + from_right[b, z].astype(F32)).astype(BF16)

        @pl.when(z == n_g - 1)
        def _():
            landed[span, :] = (part[b, z] + from_left[b, z].astype(F32)).astype(BF16)

        @pl.when(inner)
        def _():
            landed[span, :] = (
                part[b, z] + from_left[b, z].astype(F32) + from_right[b, z].astype(F32)
            ).astype(BF16)

    def drain(b, carry):
        @pl.when(z > 0)
        def _():
            own_left(b).wait_send()

        @pl.when(z < n_g - 1)
        def _():
            own_right(b).wait_send()

        for s in range(n_g):
            @pl.when(((s < z) & (z < n_g - 1)) | ((s > z) & (z > 0)))
            def _():
                feature_copy(s, b, fwd_sem.at[b, s], z).wait_send()

            @pl.when(s > z)
            def _():
                row_copy(b, s, True).wait_send()

            @pl.when(s < z)
            def _():
                row_copy(b, s, False).wait_send()

        return carry

    lax.fori_loop(0, nb, drain, 0)
    for which in range(2):
        for phase, group in groups:
            weight_whole(which, phase, group).wait_send()
        for phase in range(n_bits):
            for group in half_groups(phase):
                half_copy(which, phase, group).wait_send()


def store(hidden, gate, up, onehot, landed, hidden_to, tokens_to, gate_to, up_to, made, sem):
    n_tok = onehot.shape[0]
    tile = n_tok // TILES
    pairs = ((hidden, hidden_to), (gate, gate_to), (up, up_to))
    copies = [pltpu.make_async_copy(*pair, sem.at[i]) for i, pair in enumerate(pairs)]
    for copy in copies:
        copy.start()
    for t in range(TILES):
        span = slice(t * tile, (t + 1) * tile)
        made[span, :] = jnp.dot(
            onehot[span, :], landed[...], preferred_element_type=F32
        ).astype(BF16)
        copies.append(
            pltpu.make_async_copy(
                made.at[span], tokens_to.at[span], sem.at[len(pairs) + t]
            )
        )
        copies[-1].start()
    for copy in copies:
        copy.wait()


def shards(n_dp, n_g, tokens, gate_w, up_w, block_rows, block_count, route_gate, grad_hidden):
    n_blocks, block_len = block_rows.shape
    nb, blk = n_blocks * CUTS, block_len // CUTS
    n_tok, fw = tokens.shape
    w_rows, width = gate_w.shape
    routed_len = nb * blk
    depth = n_dp * w_rows
    n_bits = n_dp.bit_length() - 1
    factor = float((n_dp * routed_len) ** (-0.5))
    dma = pltpu.SemaphoreType.DMA
    vmem = pl.BlockSpec(memory_space=pltpu.VMEM)
    hbm = pl.BlockSpec(memory_space=pltpu.HBM)
    outs = (
        ((routed_len, width), BF16),
        ((w_rows, width), F32),
        ((w_rows, width), F32),
        ((n_tok, routed_len), BF16),
        ((routed_len, fw), BF16),
    )
    kept = sum(shape[0] * shape[1] * jnp.dtype(kind).itemsize for shape, kind in outs)
    made = pl.pallas_call(
        functools.partial(kernel, n_dp, n_g, factor),
        out_shape=tuple(pltpu.VMEM(shape, kind) for shape, kind in outs),
        in_specs=[hbm] * 7,
        out_specs=(vmem,) * len(outs),
        scratch_shapes=[
            pltpu.VMEM((n_tok, fw), BF16),
            pltpu.VMEM((n_blocks, block_len), jnp.int32),
            pltpu.VMEM((n_blocks, block_len), F32),
            pltpu.SMEM((1,), jnp.int32),
            pltpu.VMEM((routed_len, width), BF16),
            pltpu.VMEM((routed_len, block_len), F32),
            pltpu.VMEM((n_g, routed_len, fw), BF16),
            pltpu.VMEM((depth, width), BF16),
            pltpu.VMEM((depth, width), BF16),
            pltpu.VMEM((routed_len, 2 * width), BF16),
            pltpu.VMEM((nb, n_g, blk, fw), F32),
            pltpu.VMEM((nb, n_g, blk, fw), BF16),
            pltpu.VMEM((nb, n_g, blk, fw), BF16),
            pltpu.VMEM((nb, n_g, blk, fw), BF16),
            pltpu.VMEM((depth, width), F32),
            pltpu.VMEM((depth, width), F32),
            pltpu.VMEM((depth, width), BF16),
            pltpu.VMEM((depth, width), BF16),
            pltpu.VMEM((depth, width), BF16),
            pltpu.VMEM((depth, width), BF16),
            dma((nb, 2)),
            dma((nb, n_g)),
            dma((nb, n_g)),
            dma((2, n_bits, n_bits)),
            dma((2, n_bits, n_bits)),
            dma((nb, n_g)),
            dma((nb, n_g)),
            dma((nb, n_g)),
            dma((2, n_bits, 4)),
            dma((2, n_bits, 4)),
            dma((7,)),
        ],
        compiler_params=pltpu.CompilerParams(
            collective_id=0, has_side_effects=True, vmem_limit_bytes=67043328 - kept
        ),
    )(tokens, gate_w, up_w, block_rows, block_count, route_gate, grad_hidden)
    return pl.pallas_call(
        store,
        out_shape=(
            jax.ShapeDtypeStruct((routed_len, width), BF16),
            jax.ShapeDtypeStruct((n_tok, fw), BF16),
            jax.ShapeDtypeStruct((w_rows, width), F32),
            jax.ShapeDtypeStruct((w_rows, width), F32),
        ),
        in_specs=[vmem] * len(outs),
        out_specs=(hbm,) * 4,
        scratch_shapes=[pltpu.VMEM((n_tok, fw), BF16), dma((3 + TILES,))],
        compiler_params=pltpu.CompilerParams(vmem_limit_bytes=8 * 2**20),
    )(*made)


def solution(mesh):
    return jax.shard_map(
        functools.partial(shards, mesh.shape["dp"], mesh.shape["group"]),
        mesh=mesh,
        in_specs=(
            P("dp", "group"),
            P("dp", "group"),
            P("dp", "group"),
            P("dp", None),
            P("dp"),
            P("dp", None),
            P("dp", "group"),
        ),
        out_specs=(P("dp", "group"), P("dp", "group"), P("dp", "group"), P("dp", "group")),
        check_vma=False,
    )
```

```python
import functools

import jax
import jax.numpy as jnp
from jax import lax
from jax.experimental import pallas as pl
from jax.experimental.pallas import tpu as pltpu
from jax.sharding import PartitionSpec as P

F32 = jnp.float32
BF16 = jnp.bfloat16
CUTS = 2
AHEAD = 4
NEAR = 2
LEAD = 2
HOP = 2
LATE = 4
LAST = 2
EARLY = 0
TILES = 4
FLOWS = (1,3,2)
PRE = (1, 2)
GO = (1, 2, 0)
BOTH = (((0,), (0,)), ((), ()))
BACK = (((1,), (1,)), ((), ()))


def kernel(
    n_dp,
    n_g,
    factor,
    tokens_in,
    gate_w,
    up_w,
    rows_in,
    count_in,
    route_in,
    grad_in,
    hidden,
    grad_gate_w,
    grad_up_w,
    onehot,
    landed,
    tokens,
    rows,
    route,
    count,
    grad_hidden,
    coef,
    routed,
    wg,
    wu,
    grads,
    part,
    outgoing,
    from_left,
    from_right,
    sum_g,
    sum_u,
    stage_g,
    stage_u,
    got_g,
    got_u,
    own_sem,
    fwd_sem,
    ag_sem,
    w_send,
    w_recv,
    rs_send,
    left_sem,
    right_sem,
    h_send,
    h_recv,
    local_sem,
):
    n_blocks, block_len = rows.shape
    nb, blk = part.shape[0], part.shape[2]
    n_tok, fw = tokens.shape
    w_rows, width = gate_w.shape
    n_bits = n_dp.bit_length() - 1
    p = lax.axis_index("dp")
    z = lax.axis_index("group")

    def bit(k):
        return (p // 2**k) % 2

    def partner(k):
        return p + 2**k - bit(k) * 2 ** (k + 1)

    upper = list(range(1, n_bits))
    orders = (upper + [0], upper[::-1] + [0])
    inner = (z > 0) & (z < n_g - 1)

    def flipped(bits):
        return p + sum((1 - 2 * bit(k)) * 2**k for k in bits)

    copies_in = [
        pltpu.make_async_copy(source, dest, local_sem.at[i])
        for i, (source, dest) in enumerate(
            (
                (tokens_in, tokens),
                (rows_in, rows),
                (route_in, route),
                (count_in, count),
                (gate_w, wg.at[pl.ds(p * w_rows, w_rows)]),
                (up_w, wu.at[pl.ds(p * w_rows, w_rows)]),
                (grad_in, grad_hidden),
            )
        )
    ]
    for copy in copies_in:
        copy.start()

    barrier = pltpu.get_barrier_semaphore()
    for k in range(n_bits):
        pl.semaphore_signal(barrier, inc=1, device_id={"dp": partner(k)})

    @pl.when(z > 0)
    def _():
        pl.semaphore_signal(barrier, inc=1, device_id={"group": z - 1})

    @pl.when(z < n_g - 1)
    def _():
        pl.semaphore_signal(barrier, inc=1, device_id={"group": z + 1})

    def pick(b):
        span = slice(b * block_len, (b + 1) * block_len)
        hot = lax.broadcasted_iota(jnp.int32, (n_tok, block_len), 0) == rows[b : b + 1, :]
        hot = jnp.where(hot, 1.0, 0.0).astype(BF16)
        onehot[:, span] = hot
        picked = lax.dot_general(hot, tokens[...], BOTH, preferred_element_type=F32)
        routed[z, span, :] = picked.astype(BF16)

    copies_in[0].wait()
    copies_in[1].wait()
    pick(0)
    sides = jnp.minimum(z, 1) + jnp.minimum(n_g - 1 - z, 1)
    pl.semaphore_wait(barrier, n_bits + sides)

    def weight_copy(which, phase, group, owner):
        source, dest = ((gate_w, wg), (up_w, wu))[which]
        place = dest.at[pl.ds(pl.multiple_of(owner * w_rows, w_rows), w_rows)]
        return pltpu.make_async_remote_copy(
            src_ref=place if group else source,
            dst_ref=place,
            send_sem=w_send.at[which, phase, group],
            recv_sem=w_recv.at[which, phase, group],
            device_id={"dp": partner(orders[which][phase])},
        )

    def weight_whole(which, phase, group):
        span = (wg, wu)[which].at[pl.ds(0, w_rows * (2 ** (group - 1) if group else 1))]
        return pltpu.make_async_remote_copy(
            src_ref=span,
            dst_ref=span,
            send_sem=w_send.at[which, phase, group],
            recv_sem=w_recv.at[which, phase, group],
            device_id={"dp": partner(orders[which][phase])},
        )

    def weight_own(phase):
        for which in range(2):
            weight_copy(which, phase, 0, p).start()

    def weight_pass(phase, group):
        for which in range(2):
            order = orders[which]
            weight_whole(which, phase, group).wait_recv()
            low = order[: group - 1] if group else []
            for later in range(phase + 1, n_bits):
                for number in range(2 ** len(low)):
                    bits = [order[phase]] + ([order[group - 1]] if group else [])
                    bits += [k for at, k in enumerate(low) if (number >> at) & 1]
                    weight_copy(which, later, phase + 1, flipped(bits)).start()

    def feature_copy(s, b, send_sem, to):
        place = routed.at[s, pl.ds(pl.multiple_of(b * blk, blk), blk)]
        return pltpu.make_async_remote_copy(
            src_ref=place,
            dst_ref=place,
            send_sem=send_sem,
            recv_sem=ag_sem.at[b, s],
            device_id={"group": to},
        )

    def own_left(b):
        return feature_copy(z, b, own_sem.at[b, 0], z - 1)

    def own_right(b):
        return feature_copy(z, b, own_sem.at[b, 1], z + 1)

    def own_start(b):
        @pl.when(z > 0)
        def _():
            own_left(b).start()

        @pl.when(z < n_g - 1)
        def _():
            own_right(b).start()

    def take(b, k):
        @pl.when(z - k >= 0)
        def _():
            feature_copy(z - k, b, fwd_sem.at[b, z - k], z).wait_recv()

            @pl.when(z < n_g - 1)
            def _():
                feature_copy(z - k, b, fwd_sem.at[b, z - k], z + 1).start()

        @pl.when(z + k < n_g)
        def _():
            feature_copy(z + k, b, fwd_sem.at[b, z + k], z).wait_recv()

            @pl.when(z > 0)
            def _():
                feature_copy(z + k, b, fwd_sem.at[b, z + k], z - 1).start()

    def gather(b):
        def own():
            @pl.when(b + AHEAD < nb)
            def _():
                own_start(b + AHEAD)

        def near():
            @pl.when(b + NEAR < nb)
            def _():
                take(b + NEAR, 1)

        def far():
            for k in range(2, n_g):
                take(b, k)

        for which in GO:
            (own, near, far)[which]()

    cuts = block_len // blk

    def own_block(b):
        for at in range(b * cuts, (b + 1) * cuts):
            if at < AHEAD:
                own_start(at)
            else:
                @pl.when(jnp.logical_not(inner))
                def _():
                    own_start(at)

    own_block(0)
    for phase in range(n_bits):
        weight_own(phase)
    for b in range(1, n_blocks):
        pick(b)
        own_block(b)
    copies_in[2].wait()
    copies_in[3].wait()
    live = lax.broadcasted_iota(jnp.int32, (n_blocks, block_len), 0) < count[0]
    weights = jnp.where(live, route[...], 0.0)
    for b in range(n_blocks):
        turned = jnp.broadcast_to(weights[b : b + 1, :], (block_len, block_len)).T
        coef[b * block_len : (b + 1) * block_len, :] = turned
    for copy in copies_in[4:]:
        copy.wait()

    groups = [(phase, group) for phase in range(n_bits) for group in range(phase + 1)]

    @pl.when(inner)
    def _():
        for b in range(NEAR):
            take(b, 1)

    early = [pair for pair in groups if pair[0] < n_bits - 1]
    for at, (phase, group) in enumerate(early):
        weight_pass(phase, group)
        for b in range(LEAD):
            if PRE[b] == at:
                @pl.when(inner)
                def _():
                    gather(b)

    for phase, group in groups[len(early) :]:
        weight_pass(phase, group)

    def block_forward(b):
        span = pl.ds(pl.multiple_of(b * blk, blk), blk)
        gate = jnp.zeros((blk, width), F32)
        up = jnp.zeros((blk, width), F32)
        for s in range(n_g):
            x = routed[s, span, :]
            gate += jnp.dot(x, wg[s * fw : (s + 1) * fw, :], preferred_element_type=F32)
            up += jnp.dot(x, wu[s * fw : (s + 1) * fw, :], preferred_element_type=F32)
        c = jnp.concatenate([coef[span, :]] * (width // coef.shape[1]), axis=1)
        sig = jax.nn.sigmoid(gate)
        act = gate * sig
        hidden[span, :] = (c * act * up).astype(BF16)
        scaled = grad_hidden[span, :].astype(F32) * c
        gg = (scaled * up * sig * (1.0 + gate * (1.0 - sig))).astype(BF16)
        gu = (scaled * act).astype(BF16)
        grads[span, :width] = gg
        grads[span, width:] = gu
        return gg, gu

    def row_copy(b, d, right):
        return pltpu.make_async_remote_copy(
            src_ref=outgoing.at[b, d],
            dst_ref=(from_left if right else from_right).at[b, d],
            send_sem=rs_send.at[b, d],
            recv_sem=(left_sem if right else right_sem).at[b, d],
            device_id={"group": z + 1 if right else z - 1},
        )

    def end_start(b, d):
        @pl.when(z == 0)
        def _():
            row_copy(b, d, True).start()

        @pl.when(z == n_g - 1)
        def _():
            row_copy(b, d, False).start()

    def block_back(b, gg, gu):
        for k in range(n_g):
            d = jnp.where(2 * z < n_g, n_g - 1 - k, k)
            place = pl.ds(pl.multiple_of(d * fw, fw), fw)
            back = lax.dot_general(gg, wg[place, :], BACK, preferred_element_type=F32)
            back += lax.dot_general(gu, wu[place, :], BACK, preferred_element_type=F32)
            part[b, d] = back
            if k < n_g - 1:
                @pl.when(jnp.logical_not(inner))
                def _():
                    outgoing[b, d] = back.astype(BF16)

            if k < n_g - 2:
                end_start(b, d)
            elif k == n_g - 2:
                @pl.when(b < nb - LATE)
                def _():
                    end_start(b, d)

    def relay(b, d, right):
        row_copy(b, d, right).wait_recv()
        come = (from_left if right else from_right)[b, d]
        outgoing[b, d] = (part[b, d] + come.astype(F32)).astype(BF16)
        row_copy(b, d, right).start()

    def flow_side(b, right):
        final = n_g - 1 if right else 0

        @pl.when(inner & (b >= 0) & (b < nb))
        def _():
            for k in range(n_g - 1, 0, -1):
                d = z + k if right else z - k
                go = (d < n_g) if right else (d >= 0)
                if k == 1:
                    go = go & ((d == final) | (b < nb - LAST))

                @pl.when(go)
                def _():
                    relay(b, d, right)

        d = z + 1 if right else z - 1

        @pl.when(inner & (b == nb - 1) & (d != final))
        def _():
            for late in range(nb - LAST, nb):
                relay(late, d, right)

    def flow_inner(s):
        flow_side(s - HOP * (z - 1), True)
        flow_side(s - HOP * (n_g - 2 - z), False)

    begin = nb - 1 - LEAD - EARLY

    def arrive(s):
        @pl.when(inner & (s + LEAD < nb))
        def _():
            gather(s + LEAD)

        @pl.when(jnp.logical_not(inner))
        def _():
            for k in range(1, n_g):
                take(s, k)

        @pl.when(s >= begin)
        def _():
            flow_inner(s - begin)

    def stage(s, carry):
        arrive(s)
        block_back(s, *block_forward(s))
        return carry

    lax.fori_loop(0, nb - 1, stage, 0)

    totals = ((sum_g, stage_g, got_g), (sum_u, stage_u, got_u))
    paths = [order[::-1] for order in orders]
    small = w_rows % 128 > 0

    def weight_grad(which, owner):
        total = totals[which][0]
        chunk = pl.ds(pl.multiple_of(owner * w_rows, w_rows), w_rows)
        if small:
            return total[chunk, :]
        per = fw // w_rows
        across = pl.ds(pl.multiple_of((owner % per) * w_rows, w_rows), w_rows)
        return lax.dot_general(
            routed[owner // per, :, across],
            grads[:, which * width : (which + 1) * width],
            BOTH,
            preferred_element_type=F32,
        )

    def half_groups(phase):
        if phase < n_bits - 2:
            return [(0, 1), (0, 0), (1, 1), (1, 0)]
        return [(0, 0), (1, 0)] if phase == n_bits - 2 else [(0, 0)]

    def half_count(phase):
        return 2 ** max(n_bits - 3 - phase, 0)

    def half_at(phase, group, i):
        start = sum(2 ** (n_bits - 1 - t) for t in range(phase))
        at = start + half_groups(phase).index(group) * half_count(phase) + i
        return slice(at * w_rows, (at + 1) * w_rows)

    def half_owner(which, phase, group, i, mine):
        path = paths[which]
        bits = [] if mine else [path[phase]]
        if phase < n_bits - 1 and group[0] == 0:
            bits.append(path[phase + 1])
        if phase < n_bits - 2 and group[1] == 1:
            bits.append(path[phase + 2])
        bits += [k for at, k in enumerate(path[phase + 3 :]) if (i >> at) & 1]
        return flipped(bits)

    def half_copy(which, phase, group):
        total, stage_ref, got = totals[which]
        at = half_at(phase, group, 0).start
        span = pl.ds(at, half_count(phase) * w_rows)
        number = half_groups(phase).index(group)
        return pltpu.make_async_remote_copy(
            src_ref=stage_ref.at[span],
            dst_ref=got.at[span],
            send_sem=h_send.at[which, phase, number],
            recv_sem=h_recv.at[which, phase, number],
            device_id={"dp": partner(paths[which][phase])},
        )

    def half_first(group):
        for which in range(2):
            for i in range(half_count(0)):
                made = weight_grad(which, half_owner(which, 0, group, i, False))
                totals[which][1][half_at(0, group, i), :] = made.astype(BF16)
            half_copy(which, 0, group).start()

    def half_keep(group):
        if small:
            return
        for which in range(2):
            for i in range(half_count(0)):
                owner = half_owner(which, 0, group, i, True)
                chunk = pl.ds(pl.multiple_of(owner * w_rows, w_rows), w_rows)
                totals[which][0][chunk, :] = weight_grad(which, owner)

    def half_begin():
        if small:
            for s in range(n_g):
                made = lax.dot_general(
                    routed[s], grads[...], BOTH, preferred_element_type=F32
                )
                sum_g[s * fw : (s + 1) * fw, :] = made[:, :width]
                sum_u[s * fw : (s + 1) * fw, :] = made[:, width:]
        for group in todo[:half]:
            half_first(group)

    def half_pass(phase, group):
        side, sub = group
        after = 1 - sub if phase < n_bits - 2 else 0
        for which in range(2):
            total, stage_ref, got = totals[which]
            half_copy(which, phase, group).wait_recv()
            for i in range(half_count(phase)):
                owner = half_owner(which, phase, group, i, True)
                chunk = pl.ds(pl.multiple_of(owner * w_rows, w_rows), w_rows)
                value = total[chunk, :] + got[half_at(phase, group, i), :].astype(F32)
                if phase == n_bits - 1:
                    (grad_gate_w, grad_up_w)[which][...] = value * factor
                elif side == 1:
                    total[chunk, :] = value
                elif phase + 1 < n_bits - 2:
                    at = half_at(phase + 1, (after, i % 2), i // 2)
                    stage_ref[at, :] = value.astype(BF16)
                else:
                    stage_ref[half_at(phase + 1, (after, 0), 0), :] = value.astype(BF16)
            if phase < n_bits - 1 and side == 0:
                for later in half_groups(phase + 1):
                    if phase == n_bits - 2 or later[0] == after:
                        half_copy(which, phase + 1, later).start()

    todo = half_groups(0)
    half = max(len(todo) // 2, 1)
    arrive(nb - 1)
    made = block_forward(nb - 1)
    half_begin()
    block_back(nb - 1, *made)
    for b in range(nb - LATE, nb):
        end_start(b, jnp.where(z == 0, 1, n_g - 2))
    steps = list(range(nb - begin, nb + HOP * (n_g - 3)))
    done = [sum(FLOWS[: phase + 1]) for phase in range(n_bits)]
    for step in steps[: done[0]]:
        flow_inner(step)
    for group in todo[:half]:
        half_keep(group)
        half_pass(0, group)
    for group in todo[half:]:
        half_first(group)
    for group in todo[half:]:
        half_keep(group)
    for group in todo[half:]:
        half_pass(0, group)
    for phase in range(1, n_bits):
        for step in steps[done[phase - 1] : done[phase]]:
            flow_inner(step)
        for group in half_groups(phase):
            half_pass(phase, group)
    for step in steps[done[-1] :]:
        flow_inner(step)

    for b in range(nb):
        @pl.when(z > 0)
        def _():
            row_copy(b, z, True).wait_recv()

        @pl.when(z < n_g - 1)
        def _():
            row_copy(b, z, False).wait_recv()

        span = slice(b * blk, (b + 1) * blk)

        @pl.when(z == 0)
        def _():
            landed[span, :] = (part[b, z] + from_right[b, z].astype(F32)).astype(BF16)

        @pl.when(z == n_g - 1)
        def _():
            landed[span, :] = (part[b, z] + from_left[b, z].astype(F32)).astype(BF16)

        @pl.when(inner)
        def _():
            landed[span, :] = (
                part[b, z] + from_left[b, z].astype(F32) + from_right[b, z].astype(F32)
            ).astype(BF16)

    def drain(b, carry):
        @pl.when(z > 0)
        def _():
            own_left(b).wait_send()

        @pl.when(z < n_g - 1)
        def _():
            own_right(b).wait_send()

        for s in range(n_g):
            @pl.when(((s < z) & (z < n_g - 1)) | ((s > z) & (z > 0)))
            def _():
                feature_copy(s, b, fwd_sem.at[b, s], z).wait_send()

            @pl.when(s > z)
            def _():
                row_copy(b, s, True).wait_send()

            @pl.when(s < z)
            def _():
                row_copy(b, s, False).wait_send()

        return carry

    lax.fori_loop(0, nb, drain, 0)
    for which in range(2):
        for phase, group in groups:
            weight_whole(which, phase, group).wait_send()
        for phase in range(n_bits):
            for group in half_groups(phase):
                half_copy(which, phase, group).wait_send()


def store(hidden, gate, up, onehot, landed, hidden_to, tokens_to, gate_to, up_to, made, sem):
    n_tok = onehot.shape[0]
    tile = n_tok // TILES
    pairs = ((hidden, hidden_to), (gate, gate_to), (up, up_to))
    copies = [pltpu.make_async_copy(*pair, sem.at[i]) for i, pair in enumerate(pairs)]
    for copy in copies:
        copy.start()
    for t in range(TILES):
        span = slice(t * tile, (t + 1) * tile)
        made[span, :] = jnp.dot(
            onehot[span, :], landed[...], preferred_element_type=F32
        ).astype(BF16)
        copies.append(
            pltpu.make_async_copy(
                made.at[span], tokens_to.at[span], sem.at[len(pairs) + t]
            )
        )
        copies[-1].start()
    for copy in copies:
        copy.wait()


def shards(n_dp, n_g, tokens, gate_w, up_w, block_rows, block_count, route_gate, grad_hidden):
    n_blocks, block_len = block_rows.shape
    nb, blk = n_blocks * CUTS, block_len // CUTS
    n_tok, fw = tokens.shape
    w_rows, width = gate_w.shape
    routed_len = nb * blk
    depth = n_dp * w_rows
    n_bits = n_dp.bit_length() - 1
    factor = float((n_dp * routed_len) ** (-0.5))
    dma = pltpu.SemaphoreType.DMA
    vmem = pl.BlockSpec(memory_space=pltpu.VMEM)
    hbm = pl.BlockSpec(memory_space=pltpu.HBM)
    outs = (
        ((routed_len, width), BF16),
        ((w_rows, width), F32),
        ((w_rows, width), F32),
        ((n_tok, routed_len), BF16),
        ((routed_len, fw), BF16),
    )
    kept = sum(shape[0] * shape[1] * jnp.dtype(kind).itemsize for shape, kind in outs)
    made = pl.pallas_call(
        functools.partial(kernel, n_dp, n_g, factor),
        out_shape=tuple(pltpu.VMEM(shape, kind) for shape, kind in outs),
        in_specs=[hbm] * 7,
        out_specs=(vmem,) * len(outs),
        scratch_shapes=[
            pltpu.VMEM((n_tok, fw), BF16),
            pltpu.VMEM((n_blocks, block_len), jnp.int32),
            pltpu.VMEM((n_blocks, block_len), F32),
            pltpu.SMEM((1,), jnp.int32),
            pltpu.VMEM((routed_len, width), BF16),
            pltpu.VMEM((routed_len, block_len), F32),
            pltpu.VMEM((n_g, routed_len, fw), BF16),
            pltpu.VMEM((depth, width), BF16),
            pltpu.VMEM((depth, width), BF16),
            pltpu.VMEM((routed_len, 2 * width), BF16),
            pltpu.VMEM((nb, n_g, blk, fw), F32),
            pltpu.VMEM((nb, n_g, blk, fw), BF16),
            pltpu.VMEM((nb, n_g, blk, fw), BF16),
            pltpu.VMEM((nb, n_g, blk, fw), BF16),
            pltpu.VMEM((depth, width), F32),
            pltpu.VMEM((depth, width), F32),
            pltpu.VMEM((depth, width), BF16),
            pltpu.VMEM((depth, width), BF16),
            pltpu.VMEM((depth, width), BF16),
            pltpu.VMEM((depth, width), BF16),
            dma((nb, 2)),
            dma((nb, n_g)),
            dma((nb, n_g)),
            dma((2, n_bits, n_bits)),
            dma((2, n_bits, n_bits)),
            dma((nb, n_g)),
            dma((nb, n_g)),
            dma((nb, n_g)),
            dma((2, n_bits, 4)),
            dma((2, n_bits, 4)),
            dma((7,)),
        ],
        compiler_params=pltpu.CompilerParams(
            collective_id=0, has_side_effects=True, vmem_limit_bytes=67043328 - kept
        ),
    )(tokens, gate_w, up_w, block_rows, block_count, route_gate, grad_hidden)
    return pl.pallas_call(
        store,
        out_shape=(
            jax.ShapeDtypeStruct((routed_len, width), BF16),
            jax.ShapeDtypeStruct((n_tok, fw), BF16),
            jax.ShapeDtypeStruct((w_rows, width), F32),
            jax.ShapeDtypeStruct((w_rows, width), F32),
        ),
        in_specs=[vmem] * len(outs),
        out_specs=(hbm,) * 4,
        scratch_shapes=[pltpu.VMEM((n_tok, fw), BF16), dma((3 + TILES,))],
        compiler_params=pltpu.CompilerParams(vmem_limit_bytes=8 * 2**20),
    )(*made)


def solution(mesh):
    return jax.shard_map(
        functools.partial(shards, mesh.shape["dp"], mesh.shape["group"]),
        mesh=mesh,
        in_specs=(
            P("dp", "group"),
            P("dp", "group"),
            P("dp", "group"),
            P("dp", None),
            P("dp"),
            P("dp", None),
            P("dp", "group"),
        ),
        out_specs=(P("dp", "group"), P("dp", "group"), P("dp", "group"), P("dp", "group")),
        check_vma=False,
    )
```

```python
import functools

import jax
import jax.numpy as jnp
from jax import lax
from jax.experimental import pallas as pl
from jax.experimental.pallas import tpu as pltpu
from jax.sharding import PartitionSpec as P

F32 = jnp.float32
BF16 = jnp.bfloat16
CUTS = 2
AHEAD = 4
NEAR = 2
LEAD = 2
HOP = 2
LATE = 4
LAST = 3
EARLY = 0
TILES = 4
FLOWS = (1,3,2)
PRE = (0,1)
GO = (1, 2, 0)
BOTH = (((0,), (0,)), ((), ()))
BACK = (((1,), (1,)), ((), ()))


def kernel(
    n_dp,
    n_g,
    factor,
    tokens_in,
    gate_w,
    up_w,
    rows_in,
    count_in,
    route_in,
    grad_in,
    hidden,
    grad_gate_w,
    grad_up_w,
    onehot,
    landed,
    tokens,
    rows,
    route,
    count,
    grad_hidden,
    coef,
    routed,
    wg,
    wu,
    grads,
    part,
    outgoing,
    from_left,
    from_right,
    sum_g,
    sum_u,
    stage_g,
    stage_u,
    got_g,
    got_u,
    own_sem,
    fwd_sem,
    ag_sem,
    w_send,
    w_recv,
    rs_send,
    left_sem,
    right_sem,
    h_send,
    h_recv,
    local_sem,
):
    n_blocks, block_len = rows.shape
    nb, blk = part.shape[0], part.shape[2]
    n_tok, fw = tokens.shape
    w_rows, width = gate_w.shape
    n_bits = n_dp.bit_length() - 1
    p = lax.axis_index("dp")
    z = lax.axis_index("group")

    def bit(k):
        return (p // 2**k) % 2

    def partner(k):
        return p + 2**k - bit(k) * 2 ** (k + 1)

    upper = list(range(1, n_bits))
    orders = (upper + [0], upper[::-1] + [0])
    inner = (z > 0) & (z < n_g - 1)

    def flipped(bits):
        return p + sum((1 - 2 * bit(k)) * 2**k for k in bits)

    copies_in = [
        pltpu.make_async_copy(source, dest, local_sem.at[i])
        for i, (source, dest) in enumerate(
            (
                (tokens_in, tokens),
                (rows_in, rows),
                (route_in, route),
                (count_in, count),
                (gate_w, wg.at[pl.ds(p * w_rows, w_rows)]),
                (up_w, wu.at[pl.ds(p * w_rows, w_rows)]),
                (grad_in, grad_hidden),
            )
        )
    ]
    for copy in copies_in:
        copy.start()

    barrier = pltpu.get_barrier_semaphore()
    for k in range(n_bits):
        pl.semaphore_signal(barrier, inc=1, device_id={"dp": partner(k)})

    @pl.when(z > 0)
    def _():
        pl.semaphore_signal(barrier, inc=1, device_id={"group": z - 1})

    @pl.when(z < n_g - 1)
    def _():
        pl.semaphore_signal(barrier, inc=1, device_id={"group": z + 1})

    def pick(b):
        span = slice(b * block_len, (b + 1) * block_len)
        hot = lax.broadcasted_iota(jnp.int32, (n_tok, block_len), 0) == rows[b : b + 1, :]
        hot = jnp.where(hot, 1.0, 0.0).astype(BF16)
        onehot[:, span] = hot
        picked = lax.dot_general(hot, tokens[...], BOTH, preferred_element_type=F32)
        routed[z, span, :] = picked.astype(BF16)

    copies_in[0].wait()
    copies_in[1].wait()
    pick(0)
    sides = jnp.minimum(z, 1) + jnp.minimum(n_g - 1 - z, 1)
    pl.semaphore_wait(barrier, n_bits + sides)

    def weight_copy(which, phase, group, owner):
        source, dest = ((gate_w, wg), (up_w, wu))[which]
        place = dest.at[pl.ds(pl.multiple_of(owner * w_rows, w_rows), w_rows)]
        return pltpu.make_async_remote_copy(
            src_ref=place if group else source,
            dst_ref=place,
            send_sem=w_send.at[which, phase, group],
            recv_sem=w_recv.at[which, phase, group],
            device_id={"dp": partner(orders[which][phase])},
        )

    def weight_whole(which, phase, group):
        span = (wg, wu)[which].at[pl.ds(0, w_rows * (2 ** (group - 1) if group else 1))]
        return pltpu.make_async_remote_copy(
            src_ref=span,
            dst_ref=span,
            send_sem=w_send.at[which, phase, group],
            recv_sem=w_recv.at[which, phase, group],
            device_id={"dp": partner(orders[which][phase])},
        )

    def weight_own(phase):
        for which in range(2):
            weight_copy(which, phase, 0, p).start()

    def weight_pass(phase, group):
        for which in range(2):
            order = orders[which]
            weight_whole(which, phase, group).wait_recv()
            low = order[: group - 1] if group else []
            for later in range(phase + 1, n_bits):
                for number in range(2 ** len(low)):
                    bits = [order[phase]] + ([order[group - 1]] if group else [])
                    bits += [k for at, k in enumerate(low) if (number >> at) & 1]
                    weight_copy(which, later, phase + 1, flipped(bits)).start()

    def feature_copy(s, b, send_sem, to):
        place = routed.at[s, pl.ds(pl.multiple_of(b * blk, blk), blk)]
        return pltpu.make_async_remote_copy(
            src_ref=place,
            dst_ref=place,
            send_sem=send_sem,
            recv_sem=ag_sem.at[b, s],
            device_id={"group": to},
        )

    def own_left(b):
        return feature_copy(z, b, own_sem.at[b, 0], z - 1)

    def own_right(b):
        return feature_copy(z, b, own_sem.at[b, 1], z + 1)

    def own_start(b):
        @pl.when(z > 0)
        def _():
            own_left(b).start()

        @pl.when(z < n_g - 1)
        def _():
            own_right(b).start()

    def take(b, k):
        @pl.when(z - k >= 0)
        def _():
            feature_copy(z - k, b, fwd_sem.at[b, z - k], z).wait_recv()

            @pl.when(z < n_g - 1)
            def _():
                feature_copy(z - k, b, fwd_sem.at[b, z - k], z + 1).start()

        @pl.when(z + k < n_g)
        def _():
            feature_copy(z + k, b, fwd_sem.at[b, z + k], z).wait_recv()

            @pl.when(z > 0)
            def _():
                feature_copy(z + k, b, fwd_sem.at[b, z + k], z - 1).start()

    def gather(b):
        def own():
            @pl.when(b + AHEAD < nb)
            def _():
                own_start(b + AHEAD)

        def near():
            @pl.when(b + NEAR < nb)
            def _():
                take(b + NEAR, 1)

        def far():
            for k in range(2, n_g):
                take(b, k)

        for which in GO:
            (own, near, far)[which]()

    cuts = block_len // blk

    def own_block(b):
        for at in range(b * cuts, (b + 1) * cuts):
            if at < AHEAD:
                own_start(at)
            else:
                @pl.when(jnp.logical_not(inner))
                def _():
                    own_start(at)

    own_block(0)
    for phase in range(n_bits):
        weight_own(phase)
    for b in range(1, n_blocks):
        pick(b)
        own_block(b)
    copies_in[2].wait()
    copies_in[3].wait()
    live = lax.broadcasted_iota(jnp.int32, (n_blocks, block_len), 0) < count[0]
    weights = jnp.where(live, route[...], 0.0)
    for b in range(n_blocks):
        turned = jnp.broadcast_to(weights[b : b + 1, :], (block_len, block_len)).T
        coef[b * block_len : (b + 1) * block_len, :] = turned
    for copy in copies_in[4:]:
        copy.wait()

    groups = [(phase, group) for phase in range(n_bits) for group in range(phase + 1)]

    @pl.when(inner)
    def _():
        for b in range(NEAR):
            take(b, 1)

    early = [pair for pair in groups if pair[0] < n_bits - 1]
    for at, (phase, group) in enumerate(early):
        weight_pass(phase, group)
        for b in range(LEAD):
            if PRE[b] == at:
                @pl.when(inner)
                def _():
                    gather(b)

    for phase, group in groups[len(early) :]:
        weight_pass(phase, group)

    def block_forward(b):
        span = pl.ds(pl.multiple_of(b * blk, blk), blk)
        gate = jnp.zeros((blk, width), F32)
        up = jnp.zeros((blk, width), F32)
        for s in range(n_g):
            x = routed[s, span, :]
            gate += jnp.dot(x, wg[s * fw : (s + 1) * fw, :], preferred_element_type=F32)
            up += jnp.dot(x, wu[s * fw : (s + 1) * fw, :], preferred_element_type=F32)
        c = jnp.concatenate([coef[span, :]] * (width // coef.shape[1]), axis=1)
        sig = jax.nn.sigmoid(gate)
        act = gate * sig
        hidden[span, :] = (c * act * up).astype(BF16)
        scaled = grad_hidden[span, :].astype(F32) * c
        gg = (scaled * up * sig * (1.0 + gate * (1.0 - sig))).astype(BF16)
        gu = (scaled * act).astype(BF16)
        grads[span, :width] = gg
        grads[span, width:] = gu
        return gg, gu

    def row_copy(b, d, right):
        return pltpu.make_async_remote_copy(
            src_ref=outgoing.at[b, d],
            dst_ref=(from_left if right else from_right).at[b, d],
            send_sem=rs_send.at[b, d],
            recv_sem=(left_sem if right else right_sem).at[b, d],
            device_id={"group": z + 1 if right else z - 1},
        )

    def end_start(b, d):
        @pl.when(z == 0)
        def _():
            row_copy(b, d, True).start()

        @pl.when(z == n_g - 1)
        def _():
            row_copy(b, d, False).start()

    def block_back(b, gg, gu):
        for k in range(n_g):
            d = jnp.where(2 * z < n_g, n_g - 1 - k, k)
            place = pl.ds(pl.multiple_of(d * fw, fw), fw)
            back = lax.dot_general(gg, wg[place, :], BACK, preferred_element_type=F32)
            back += lax.dot_general(gu, wu[place, :], BACK, preferred_element_type=F32)
            part[b, d] = back
            if k < n_g - 1:
                @pl.when(jnp.logical_not(inner))
                def _():
                    outgoing[b, d] = back.astype(BF16)

            if k < n_g - 2:
                end_start(b, d)
            elif k == n_g - 2:
                @pl.when(b < nb - LATE)
                def _():
                    end_start(b, d)

    def relay(b, d, right):
        row_copy(b, d, right).wait_recv()
        come = (from_left if right else from_right)[b, d]
        outgoing[b, d] = (part[b, d] + come.astype(F32)).astype(BF16)
        row_copy(b, d, right).start()

    def flow_side(b, right):
        final = n_g - 1 if right else 0

        @pl.when(inner & (b >= 0) & (b < nb))
        def _():
            for k in range(n_g - 1, 0, -1):
                d = z + k if right else z - k
                go = (d < n_g) if right else (d >= 0)
                if k == 1:
                    go = go & ((d == final) | (b < nb - LAST))

                @pl.when(go)
                def _():
                    relay(b, d, right)

        d = z + 1 if right else z - 1

        @pl.when(inner & (b == nb - 1) & (d != final))
        def _():
            for late in range(nb - LAST, nb):
                relay(late, d, right)

    def flow_inner(s):
        flow_side(s - HOP * (z - 1), True)
        flow_side(s - HOP * (n_g - 2 - z), False)

    begin = nb - 1 - LEAD - EARLY

    def arrive(s):
        @pl.when(inner & (s + LEAD < nb))
        def _():
            gather(s + LEAD)

        @pl.when(jnp.logical_not(inner))
        def _():
            for k in range(1, n_g):
                take(s, k)

        @pl.when(s >= begin)
        def _():
            flow_inner(s - begin)

    def stage(s, carry):
        arrive(s)
        block_back(s, *block_forward(s))
        return carry

    lax.fori_loop(0, nb - 1, stage, 0)

    totals = ((sum_g, stage_g, got_g), (sum_u, stage_u, got_u))
    paths = [order[::-1] for order in orders]
    small = w_rows % 128 > 0

    def weight_grad(which, owner):
        total = totals[which][0]
        chunk = pl.ds(pl.multiple_of(owner * w_rows, w_rows), w_rows)
        if small:
            return total[chunk, :]
        per = fw // w_rows
        across = pl.ds(pl.multiple_of((owner % per) * w_rows, w_rows), w_rows)
        return lax.dot_general(
            routed[owner // per, :, across],
            grads[:, which * width : (which + 1) * width],
            BOTH,
            preferred_element_type=F32,
        )

    def half_groups(phase):
        if phase < n_bits - 2:
            return [(0, 1), (0, 0), (1, 1), (1, 0)]
        return [(0, 0), (1, 0)] if phase == n_bits - 2 else [(0, 0)]

    def half_count(phase):
        return 2 ** max(n_bits - 3 - phase, 0)

    def half_at(phase, group, i):
        start = sum(2 ** (n_bits - 1 - t) for t in range(phase))
        at = start + half_groups(phase).index(group) * half_count(phase) + i
        return slice(at * w_rows, (at + 1) * w_rows)

    def half_owner(which, phase, group, i, mine):
        path = paths[which]
        bits = [] if mine else [path[phase]]
        if phase < n_bits - 1 and group[0] == 0:
            bits.append(path[phase + 1])
        if phase < n_bits - 2 and group[1] == 1:
            bits.append(path[phase + 2])
        bits += [k for at, k in enumerate(path[phase + 3 :]) if (i >> at) & 1]
        return flipped(bits)

    def half_copy(which, phase, group):
        total, stage_ref, got = totals[which]
        at = half_at(phase, group, 0).start
        span = pl.ds(at, half_count(phase) * w_rows)
        number = half_groups(phase).index(group)
        return pltpu.make_async_remote_copy(
            src_ref=stage_ref.at[span],
            dst_ref=got.at[span],
            send_sem=h_send.at[which, phase, number],
            recv_sem=h_recv.at[which, phase, number],
            device_id={"dp": partner(paths[which][phase])},
        )

    def half_first(group):
        for which in range(2):
            for i in range(half_count(0)):
                made = weight_grad(which, half_owner(which, 0, group, i, False))
                totals[which][1][half_at(0, group, i), :] = made.astype(BF16)
            half_copy(which, 0, group).start()

    def half_keep(group):
        if small:
            return
        for which in range(2):
            for i in range(half_count(0)):
                owner = half_owner(which, 0, group, i, True)
                chunk = pl.ds(pl.multiple_of(owner * w_rows, w_rows), w_rows)
                totals[which][0][chunk, :] = weight_grad(which, owner)

    def half_begin():
        if small:
            for s in range(n_g):
                made = lax.dot_general(
                    routed[s], grads[...], BOTH, preferred_element_type=F32
                )
                sum_g[s * fw : (s + 1) * fw, :] = made[:, :width]
                sum_u[s * fw : (s + 1) * fw, :] = made[:, width:]
        for group in todo[:half]:
            half_first(group)

    def half_pass(phase, group):
        side, sub = group
        after = 1 - sub if phase < n_bits - 2 else 0
        for which in range(2):
            total, stage_ref, got = totals[which]
            half_copy(which, phase, group).wait_recv()
            for i in range(half_count(phase)):
                owner = half_owner(which, phase, group, i, True)
                chunk = pl.ds(pl.multiple_of(owner * w_rows, w_rows), w_rows)
                value = total[chunk, :] + got[half_at(phase, group, i), :].astype(F32)
                if phase == n_bits - 1:
                    (grad_gate_w, grad_up_w)[which][...] = value * factor
                elif side == 1:
                    total[chunk, :] = value
                elif phase + 1 < n_bits - 2:
                    at = half_at(phase + 1, (after, i % 2), i // 2)
                    stage_ref[at, :] = value.astype(BF16)
                else:
                    stage_ref[half_at(phase + 1, (after, 0), 0), :] = value.astype(BF16)
            if phase < n_bits - 1 and side == 0:
                for later in half_groups(phase + 1):
                    if phase == n_bits - 2 or later[0] == after:
                        half_copy(which, phase + 1, later).start()

    todo = half_groups(0)
    half = max(len(todo) // 2, 1)
    arrive(nb - 1)
    made = block_forward(nb - 1)
    half_begin()
    block_back(nb - 1, *made)
    for b in range(nb - LATE, nb):
        end_start(b, jnp.where(z == 0, 1, n_g - 2))
    steps = list(range(nb - begin, nb + HOP * (n_g - 3)))
    def land(b):
        @pl.when(z > 0)
        def _():
            row_copy(b, z, True).wait_recv()

        @pl.when(z < n_g - 1)
        def _():
            row_copy(b, z, False).wait_recv()

        span = slice(b * blk, (b + 1) * blk)

        @pl.when(z == 0)
        def _():
            landed[span, :] = (part[b, z] + from_right[b, z].astype(F32)).astype(BF16)

        @pl.when(z == n_g - 1)
        def _():
            landed[span, :] = (part[b, z] + from_left[b, z].astype(F32)).astype(BF16)

        @pl.when(inner)
        def _():
            landed[span, :] = (
                part[b, z] + from_left[b, z].astype(F32) + from_right[b, z].astype(F32)
            ).astype(BF16)

    def feature_drain(b, carry):
        @pl.when(z > 0)
        def _():
            own_left(b).wait_send()

        @pl.when(z < n_g - 1)
        def _():
            own_right(b).wait_send()

        for s in range(n_g):
            @pl.when(((s < z) & (z < n_g - 1)) | ((s > z) & (z > 0)))
            def _():
                feature_copy(s, b, fwd_sem.at[b, s], z).wait_send()

        return carry

    def early_drain():
        lax.fori_loop(0, nb, feature_drain, 0)
        for which in range(2):
            for phase, group in groups:
                weight_whole(which, phase, group).wait_send()

    done = [sum(FLOWS[: phase + 1]) for phase in range(n_bits)]
    for step in steps[: done[0]]:
        flow_inner(step)
    for group in todo[:half]:
        half_keep(group)
        half_pass(0, group)
    for group in todo[half:]:
        half_first(group)
    for group in todo[half:]:
        half_keep(group)
    for group in todo[half:]:
        half_pass(0, group)
    for phase in range(1, n_bits):
        for step in steps[done[phase - 1] : done[phase]]:
            flow_inner(step)
        if phase == n_bits - 1:
            early_drain()
            for b in range(nb - LATE):
                land(b)
        for group in half_groups(phase):
            half_pass(phase, group)
    for step in steps[done[-1] :]:
        flow_inner(step)

    for b in range(nb - LATE, nb):
        land(b)

    def row_drain(b, carry):
        for s in range(n_g):
            @pl.when(s > z)
            def _():
                row_copy(b, s, True).wait_send()

            @pl.when(s < z)
            def _():
                row_copy(b, s, False).wait_send()

        return carry

    lax.fori_loop(0, nb, row_drain, 0)
    for which in range(2):
        for phase in range(n_bits):
            for group in half_groups(phase):
                half_copy(which, phase, group).wait_send()


def store(hidden, gate, up, onehot, landed, hidden_to, tokens_to, gate_to, up_to, made, sem):
    n_tok = onehot.shape[0]
    tile = n_tok // TILES
    pairs = ((hidden, hidden_to), (gate, gate_to), (up, up_to))
    copies = [pltpu.make_async_copy(*pair, sem.at[i]) for i, pair in enumerate(pairs)]
    for copy in copies:
        copy.start()
    for t in range(TILES):
        span = slice(t * tile, (t + 1) * tile)
        made[span, :] = jnp.dot(
            onehot[span, :], landed[...], preferred_element_type=F32
        ).astype(BF16)
        copies.append(
            pltpu.make_async_copy(
                made.at[span], tokens_to.at[span], sem.at[len(pairs) + t]
            )
        )
        copies[-1].start()
    for copy in copies:
        copy.wait()


def shards(n_dp, n_g, tokens, gate_w, up_w, block_rows, block_count, route_gate, grad_hidden):
    n_blocks, block_len = block_rows.shape
    nb, blk = n_blocks * CUTS, block_len // CUTS
    n_tok, fw = tokens.shape
    w_rows, width = gate_w.shape
    routed_len = nb * blk
    depth = n_dp * w_rows
    n_bits = n_dp.bit_length() - 1
    factor = float((n_dp * routed_len) ** (-0.5))
    dma = pltpu.SemaphoreType.DMA
    vmem = pl.BlockSpec(memory_space=pltpu.VMEM)
    hbm = pl.BlockSpec(memory_space=pltpu.HBM)
    outs = (
        ((routed_len, width), BF16),
        ((w_rows, width), F32),
        ((w_rows, width), F32),
        ((n_tok, routed_len), BF16),
        ((routed_len, fw), BF16),
    )
    kept = sum(shape[0] * shape[1] * jnp.dtype(kind).itemsize for shape, kind in outs)
    made = pl.pallas_call(
        functools.partial(kernel, n_dp, n_g, factor),
        out_shape=tuple(pltpu.VMEM(shape, kind) for shape, kind in outs),
        in_specs=[hbm] * 7,
        out_specs=(vmem,) * len(outs),
        scratch_shapes=[
            pltpu.VMEM((n_tok, fw), BF16),
            pltpu.VMEM((n_blocks, block_len), jnp.int32),
            pltpu.VMEM((n_blocks, block_len), F32),
            pltpu.SMEM((1,), jnp.int32),
            pltpu.VMEM((routed_len, width), BF16),
            pltpu.VMEM((routed_len, block_len), F32),
            pltpu.VMEM((n_g, routed_len, fw), BF16),
            pltpu.VMEM((depth, width), BF16),
            pltpu.VMEM((depth, width), BF16),
            pltpu.VMEM((routed_len, 2 * width), BF16),
            pltpu.VMEM((nb, n_g, blk, fw), F32),
            pltpu.VMEM((nb, n_g, blk, fw), BF16),
            pltpu.VMEM((nb, n_g, blk, fw), BF16),
            pltpu.VMEM((nb, n_g, blk, fw), BF16),
            pltpu.VMEM((depth, width), F32),
            pltpu.VMEM((depth, width), F32),
            pltpu.VMEM((depth, width), BF16),
            pltpu.VMEM((depth, width), BF16),
            pltpu.VMEM((depth, width), BF16),
            pltpu.VMEM((depth, width), BF16),
            dma((nb, 2)),
            dma((nb, n_g)),
            dma((nb, n_g)),
            dma((2, n_bits, n_bits)),
            dma((2, n_bits, n_bits)),
            dma((nb, n_g)),
            dma((nb, n_g)),
            dma((nb, n_g)),
            dma((2, n_bits, 4)),
            dma((2, n_bits, 4)),
            dma((7,)),
        ],
        compiler_params=pltpu.CompilerParams(
            collective_id=0, has_side_effects=True, vmem_limit_bytes=67043328 - kept
        ),
    )(tokens, gate_w, up_w, block_rows, block_count, route_gate, grad_hidden)
    return pl.pallas_call(
        store,
        out_shape=(
            jax.ShapeDtypeStruct((routed_len, width), BF16),
            jax.ShapeDtypeStruct((n_tok, fw), BF16),
            jax.ShapeDtypeStruct((w_rows, width), F32),
            jax.ShapeDtypeStruct((w_rows, width), F32),
        ),
        in_specs=[vmem] * len(outs),
        out_specs=(hbm,) * 4,
        scratch_shapes=[pltpu.VMEM((n_tok, fw), BF16), dma((3 + TILES,))],
        compiler_params=pltpu.CompilerParams(vmem_limit_bytes=8 * 2**20),
    )(*made)


def solution(mesh):
    return jax.shard_map(
        functools.partial(shards, mesh.shape["dp"], mesh.shape["group"]),
        mesh=mesh,
        in_specs=(
            P("dp", "group"),
            P("dp", "group"),
            P("dp", "group"),
            P("dp", None),
            P("dp"),
            P("dp", None),
            P("dp", "group"),
        ),
        out_specs=(P("dp", "group"), P("dp", "group"), P("dp", "group"), P("dp", "group")),
        check_vma=False,
    )
```

```python
import functools

import jax
import jax.numpy as jnp
from jax import lax
from jax.experimental import pallas as pl
from jax.experimental.pallas import tpu as pltpu
from jax.sharding import PartitionSpec as P

F32 = jnp.float32
BF16 = jnp.bfloat16
CUTS = 2
AHEAD = 4
NEAR = 2
LEAD = 2
HOP = 2
LATE = 4
LAST = 3
EARLY = 0
TILES = 4
FLOWS = (1,3,2)
PRE = (0,1)
GO = (1, 2, 0)
BOTH = (((0,), (0,)), ((), ()))
BACK = (((1,), (1,)), ((), ()))


def kernel(
    n_dp,
    n_g,
    factor,
    tokens_in,
    gate_w,
    up_w,
    rows_in,
    count,
    route_in,
    grad_in,
    hidden,
    grad_gate_w,
    grad_up_w,
    onehot,
    landed,
    tokens,
    rows,
    route,
    grad_hidden,
    coef,
    routed,
    wg,
    wu,
    grads,
    part,
    outgoing,
    from_left,
    from_right,
    sum_g,
    sum_u,
    stage_g,
    stage_u,
    got_g,
    got_u,
    own_sem,
    fwd_sem,
    ag_sem,
    w_send,
    w_recv,
    rs_send,
    left_sem,
    right_sem,
    h_send,
    h_recv,
    local_sem,
):
    n_blocks, block_len = rows.shape
    nb, blk = part.shape[0], part.shape[2]
    n_tok, fw = tokens.shape
    w_rows, width = gate_w.shape
    n_bits = n_dp.bit_length() - 1
    p = lax.axis_index("dp")
    z = lax.axis_index("group")

    def bit(k):
        return (p // 2**k) % 2

    def partner(k):
        return p + 2**k - bit(k) * 2 ** (k + 1)

    upper = list(range(1, n_bits))
    orders = (upper + [0], upper[::-1] + [0])
    inner = (z > 0) & (z < n_g - 1)

    def flipped(bits):
        return p + sum((1 - 2 * bit(k)) * 2**k for k in bits)

    copies_in = [
        pltpu.make_async_copy(source, dest, local_sem.at[i])
        for i, (source, dest) in enumerate(
            (
                (tokens_in, tokens),
                (rows_in, rows),
                (route_in, route),
                (gate_w, wg.at[pl.ds(p * w_rows, w_rows)]),
                (up_w, wu.at[pl.ds(p * w_rows, w_rows)]),
                (grad_in, grad_hidden),
            )
        )
    ]
    for copy in copies_in:
        copy.start()

    barrier = pltpu.get_barrier_semaphore()
    for k in range(n_bits):
        pl.semaphore_signal(barrier, inc=1, device_id={"dp": partner(k)})

    @pl.when(z > 0)
    def _():
        pl.semaphore_signal(barrier, inc=1, device_id={"group": z - 1})

    @pl.when(z < n_g - 1)
    def _():
        pl.semaphore_signal(barrier, inc=1, device_id={"group": z + 1})

    def pick(b):
        span = slice(b * block_len, (b + 1) * block_len)
        hot = lax.broadcasted_iota(jnp.int32, (n_tok, block_len), 0) == rows[b : b + 1, :]
        hot = jnp.where(hot, 1.0, 0.0).astype(BF16)
        onehot[:, span] = hot
        picked = lax.dot_general(hot, tokens[...], BOTH, preferred_element_type=F32)
        routed[z, span, :] = picked.astype(BF16)

    copies_in[0].wait()
    copies_in[1].wait()
    pick(0)
    sides = jnp.minimum(z, 1) + jnp.minimum(n_g - 1 - z, 1)
    pl.semaphore_wait(barrier, n_bits + sides)

    def weight_copy(which, phase, group, owner):
        source, dest = ((gate_w, wg), (up_w, wu))[which]
        place = dest.at[pl.ds(pl.multiple_of(owner * w_rows, w_rows), w_rows)]
        return pltpu.make_async_remote_copy(
            src_ref=place if group else source,
            dst_ref=place,
            send_sem=w_send.at[which, phase, group],
            recv_sem=w_recv.at[which, phase, group],
            device_id={"dp": partner(orders[which][phase])},
        )

    def weight_whole(which, phase, group):
        span = (wg, wu)[which].at[pl.ds(0, w_rows * (2 ** (group - 1) if group else 1))]
        return pltpu.make_async_remote_copy(
            src_ref=span,
            dst_ref=span,
            send_sem=w_send.at[which, phase, group],
            recv_sem=w_recv.at[which, phase, group],
            device_id={"dp": partner(orders[which][phase])},
        )

    def weight_own(phase):
        for which in range(2):
            weight_copy(which, phase, 0, p).start()

    def weight_pass(phase, group):
        for which in range(2):
            order = orders[which]
            weight_whole(which, phase, group).wait_recv()
            low = order[: group - 1] if group else []
            for later in range(phase + 1, n_bits):
                for number in range(2 ** len(low)):
                    bits = [order[phase]] + ([order[group - 1]] if group else [])
                    bits += [k for at, k in enumerate(low) if (number >> at) & 1]
                    weight_copy(which, later, phase + 1, flipped(bits)).start()

    def feature_copy(s, b, send_sem, to):
        place = routed.at[s, pl.ds(pl.multiple_of(b * blk, blk), blk)]
        return pltpu.make_async_remote_copy(
            src_ref=place,
            dst_ref=place,
            send_sem=send_sem,
            recv_sem=ag_sem.at[b, s],
            device_id={"group": to},
        )

    def own_left(b):
        return feature_copy(z, b, own_sem.at[b, 0], z - 1)

    def own_right(b):
        return feature_copy(z, b, own_sem.at[b, 1], z + 1)

    def own_start(b):
        @pl.when(z > 0)
        def _():
            own_left(b).start()

        @pl.when(z < n_g - 1)
        def _():
            own_right(b).start()

    def take(b, k):
        @pl.when(z - k >= 0)
        def _():
            feature_copy(z - k, b, fwd_sem.at[b, z - k], z).wait_recv()

            @pl.when(z < n_g - 1)
            def _():
                feature_copy(z - k, b, fwd_sem.at[b, z - k], z + 1).start()

        @pl.when(z + k < n_g)
        def _():
            feature_copy(z + k, b, fwd_sem.at[b, z + k], z).wait_recv()

            @pl.when(z > 0)
            def _():
                feature_copy(z + k, b, fwd_sem.at[b, z + k], z - 1).start()

    def gather(b):
        def own():
            @pl.when(b + AHEAD < nb)
            def _():
                own_start(b + AHEAD)

        def near():
            @pl.when(b + NEAR < nb)
            def _():
                take(b + NEAR, 1)

        def far():
            for k in range(2, n_g):
                take(b, k)

        for which in GO:
            (own, near, far)[which]()

    cuts = block_len // blk

    def own_block(b):
        for at in range(b * cuts, (b + 1) * cuts):
            if at < AHEAD:
                own_start(at)
            else:
                @pl.when(jnp.logical_not(inner))
                def _():
                    own_start(at)

    own_block(0)
    for phase in range(n_bits):
        weight_own(phase)
    for b in range(1, n_blocks):
        pick(b)
        own_block(b)
    copies_in[2].wait()
    live = lax.broadcasted_iota(jnp.int32, (n_blocks, block_len), 0) < count[0]
    weights = jnp.where(live, route[...], 0.0)
    for b in range(n_blocks):
        turned = jnp.broadcast_to(weights[b : b + 1, :], (block_len, block_len)).T
        coef[b * block_len : (b + 1) * block_len, :] = turned
    for copy in copies_in[3:]:
        copy.wait()

    groups = [(phase, group) for phase in range(n_bits) for group in range(phase + 1)]

    @pl.when(inner)
    def _():
        for b in range(NEAR):
            take(b, 1)

    early = [pair for pair in groups if pair[0] < n_bits - 1]
    for at, (phase, group) in enumerate(early):
        weight_pass(phase, group)
        for b in range(LEAD):
            if PRE[b] == at:
                @pl.when(inner)
                def _():
                    gather(b)

    for phase, group in groups[len(early) :]:
        weight_pass(phase, group)

    def block_forward(b):
        span = pl.ds(pl.multiple_of(b * blk, blk), blk)
        gate = jnp.zeros((blk, width), F32)
        up = jnp.zeros((blk, width), F32)
        for s in range(n_g):
            x = routed[s, span, :]
            gate += jnp.dot(x, wg[s * fw : (s + 1) * fw, :], preferred_element_type=F32)
            up += jnp.dot(x, wu[s * fw : (s + 1) * fw, :], preferred_element_type=F32)
        c = jnp.concatenate([coef[span, :]] * (width // coef.shape[1]), axis=1)
        sig = jax.nn.sigmoid(gate)
        act = gate * sig
        hidden[span, :] = (c * act * up).astype(BF16)
        scaled = grad_hidden[span, :].astype(F32) * c
        gg = (scaled * up * sig * (1.0 + gate * (1.0 - sig))).astype(BF16)
        gu = (scaled * act).astype(BF16)
        grads[span, :width] = gg
        grads[span, width:] = gu
        return gg, gu

    def row_copy(b, d, right):
        return pltpu.make_async_remote_copy(
            src_ref=outgoing.at[b, d],
            dst_ref=(from_left if right else from_right).at[b, d],
            send_sem=rs_send.at[b, d],
            recv_sem=(left_sem if right else right_sem).at[b, d],
            device_id={"group": z + 1 if right else z - 1},
        )

    def end_start(b, d):
        @pl.when(z == 0)
        def _():
            row_copy(b, d, True).start()

        @pl.when(z == n_g - 1)
        def _():
            row_copy(b, d, False).start()

    def block_back(b, gg, gu):
        for k in range(n_g):
            d = jnp.where(2 * z < n_g, n_g - 1 - k, k)
            place = pl.ds(pl.multiple_of(d * fw, fw), fw)
            back = lax.dot_general(gg, wg[place, :], BACK, preferred_element_type=F32)
            back += lax.dot_general(gu, wu[place, :], BACK, preferred_element_type=F32)
            part[b, d] = back
            if k < n_g - 1:
                @pl.when(jnp.logical_not(inner))
                def _():
                    outgoing[b, d] = back.astype(BF16)

            if k < n_g - 2:
                end_start(b, d)
            elif k == n_g - 2:
                @pl.when(b < nb - LATE)
                def _():
                    end_start(b, d)

    def relay(b, d, right):
        row_copy(b, d, right).wait_recv()
        come = (from_left if right else from_right)[b, d]
        outgoing[b, d] = (part[b, d] + come.astype(F32)).astype(BF16)
        row_copy(b, d, right).start()

    def flow_side(b, right):
        final = n_g - 1 if right else 0

        @pl.when(inner & (b >= 0) & (b < nb))
        def _():
            for k in range(n_g - 1, 0, -1):
                d = z + k if right else z - k
                go = (d < n_g) if right else (d >= 0)
                if k == 1:
                    go = go & ((d == final) | (b < nb - LAST))

                @pl.when(go)
                def _():
                    relay(b, d, right)

        d = z + 1 if right else z - 1

        @pl.when(inner & (b == nb - 1) & (d != final))
        def _():
            for late in range(nb - LAST, nb):
                relay(late, d, right)

    def flow_inner(s):
        flow_side(s - HOP * (z - 1), True)
        flow_side(s - HOP * (n_g - 2 - z), False)

    begin = nb - 1 - LEAD - EARLY

    def arrive(s):
        @pl.when(inner & (s + LEAD < nb))
        def _():
            gather(s + LEAD)

        @pl.when(jnp.logical_not(inner))
        def _():
            for k in range(1, n_g):
                take(s, k)

        @pl.when(s >= begin)
        def _():
            flow_inner(s - begin)

    def stage(s, carry):
        arrive(s)
        block_back(s, *block_forward(s))
        return carry

    lax.fori_loop(0, nb - 1, stage, 0)

    totals = ((sum_g, stage_g, got_g), (sum_u, stage_u, got_u))
    paths = [order[::-1] for order in orders]
    small = w_rows % 128 > 0

    def weight_grad(which, owner):
        total = totals[which][0]
        chunk = pl.ds(pl.multiple_of(owner * w_rows, w_rows), w_rows)
        if small:
            return total[chunk, :]
        per = fw // w_rows
        across = pl.ds(pl.multiple_of((owner % per) * w_rows, w_rows), w_rows)
        return lax.dot_general(
            routed[owner // per, :, across],
            grads[:, which * width : (which + 1) * width],
            BOTH,
            preferred_element_type=F32,
        )

    def half_groups(phase):
        if phase < n_bits - 2:
            return [(0, 1), (0, 0), (1, 1), (1, 0)]
        return [(0, 0), (1, 0)] if phase == n_bits - 2 else [(0, 0)]

    def half_count(phase):
        return 2 ** max(n_bits - 3 - phase, 0)

    def half_at(phase, group, i):
        start = sum(2 ** (n_bits - 1 - t) for t in range(phase))
        at = start + half_groups(phase).index(group) * half_count(phase) + i
        return slice(at * w_rows, (at + 1) * w_rows)

    def half_owner(which, phase, group, i, mine):
        path = paths[which]
        bits = [] if mine else [path[phase]]
        if phase < n_bits - 1 and group[0] == 0:
            bits.append(path[phase + 1])
        if phase < n_bits - 2 and group[1] == 1:
            bits.append(path[phase + 2])
        bits += [k for at, k in enumerate(path[phase + 3 :]) if (i >> at) & 1]
        return flipped(bits)

    def half_copy(which, phase, group):
        total, stage_ref, got = totals[which]
        at = half_at(phase, group, 0).start
        span = pl.ds(at, half_count(phase) * w_rows)
        number = half_groups(phase).index(group)
        return pltpu.make_async_remote_copy(
            src_ref=stage_ref.at[span],
            dst_ref=got.at[span],
            send_sem=h_send.at[which, phase, number],
            recv_sem=h_recv.at[which, phase, number],
            device_id={"dp": partner(paths[which][phase])},
        )

    def half_first(group):
        for which in range(2):
            for i in range(half_count(0)):
                made = weight_grad(which, half_owner(which, 0, group, i, False))
                totals[which][1][half_at(0, group, i), :] = made.astype(BF16)
            half_copy(which, 0, group).start()

    def half_keep(group):
        if small:
            return
        for which in range(2):
            for i in range(half_count(0)):
                owner = half_owner(which, 0, group, i, True)
                chunk = pl.ds(pl.multiple_of(owner * w_rows, w_rows), w_rows)
                totals[which][0][chunk, :] = weight_grad(which, owner)

    def half_begin():
        if small:
            for s in range(n_g):
                made = lax.dot_general(
                    routed[s], grads[...], BOTH, preferred_element_type=F32
                )
                sum_g[s * fw : (s + 1) * fw, :] = made[:, :width]
                sum_u[s * fw : (s + 1) * fw, :] = made[:, width:]
        for group in todo[:half]:
            half_first(group)

    def half_pass(phase, group):
        side, sub = group
        after = 1 - sub if phase < n_bits - 2 else 0
        for which in range(2):
            total, stage_ref, got = totals[which]
            half_copy(which, phase, group).wait_recv()
            for i in range(half_count(phase)):
                owner = half_owner(which, phase, group, i, True)
                chunk = pl.ds(pl.multiple_of(owner * w_rows, w_rows), w_rows)
                value = total[chunk, :] + got[half_at(phase, group, i), :].astype(F32)
                if phase == n_bits - 1:
                    (grad_gate_w, grad_up_w)[which][...] = value * factor
                elif side == 1:
                    total[chunk, :] = value
                elif phase + 1 < n_bits - 2:
                    at = half_at(phase + 1, (after, i % 2), i // 2)
                    stage_ref[at, :] = value.astype(BF16)
                else:
                    stage_ref[half_at(phase + 1, (after, 0), 0), :] = value.astype(BF16)
            if phase < n_bits - 1 and side == 0:
                for later in half_groups(phase + 1):
                    if phase == n_bits - 2 or later[0] == after:
                        half_copy(which, phase + 1, later).start()

    todo = half_groups(0)
    half = max(len(todo) // 2, 1)
    arrive(nb - 1)
    made = block_forward(nb - 1)
    half_begin()
    block_back(nb - 1, *made)
    for b in range(nb - LATE, nb):
        end_start(b, jnp.where(z == 0, 1, n_g - 2))
    steps = list(range(nb - begin, nb + HOP * (n_g - 3)))
    def land(b):
        @pl.when(z > 0)
        def _():
            row_copy(b, z, True).wait_recv()

        @pl.when(z < n_g - 1)
        def _():
            row_copy(b, z, False).wait_recv()

        span = slice(b * blk, (b + 1) * blk)

        @pl.when(z == 0)
        def _():
            landed[span, :] = (part[b, z] + from_right[b, z].astype(F32)).astype(BF16)

        @pl.when(z == n_g - 1)
        def _():
            landed[span, :] = (part[b, z] + from_left[b, z].astype(F32)).astype(BF16)

        @pl.when(inner)
        def _():
            landed[span, :] = (
                part[b, z] + from_left[b, z].astype(F32) + from_right[b, z].astype(F32)
            ).astype(BF16)

    def feature_drain(b, carry):
        @pl.when(z > 0)
        def _():
            own_left(b).wait_send()

        @pl.when(z < n_g - 1)
        def _():
            own_right(b).wait_send()

        for s in range(n_g):
            @pl.when(((s < z) & (z < n_g - 1)) | ((s > z) & (z > 0)))
            def _():
                feature_copy(s, b, fwd_sem.at[b, s], z).wait_send()

        return carry

    def early_drain():
        lax.fori_loop(0, nb, feature_drain, 0)
        for which in range(2):
            for phase, group in groups:
                weight_whole(which, phase, group).wait_send()

    done = [sum(FLOWS[: phase + 1]) for phase in range(n_bits)]
    for step in steps[: done[0]]:
        flow_inner(step)
    for group in todo[:half]:
        half_keep(group)
        half_pass(0, group)
    for group in todo[half:]:
        half_first(group)
    for group in todo[half:]:
        half_keep(group)
    for group in todo[half:]:
        half_pass(0, group)
    for phase in range(1, n_bits):
        for step in steps[done[phase - 1] : done[phase]]:
            flow_inner(step)
        if phase == n_bits - 1:
            early_drain()
            for b in range(nb - LATE):
                land(b)
        for group in half_groups(phase):
            half_pass(phase, group)
    for step in steps[done[-1] :]:
        flow_inner(step)

    for b in range(nb - LATE, nb):
        land(b)

    def row_drain(b, carry):
        for s in range(n_g):
            @pl.when(s > z)
            def _():
                row_copy(b, s, True).wait_send()

            @pl.when(s < z)
            def _():
                row_copy(b, s, False).wait_send()

        return carry

    lax.fori_loop(0, nb, row_drain, 0)
    for which in range(2):
        for phase in range(n_bits):
            for group in half_groups(phase):
                half_copy(which, phase, group).wait_send()


def store(hidden, gate, up, onehot, landed, hidden_to, tokens_to, gate_to, up_to, made, sem):
    n_tok = onehot.shape[0]
    tile = n_tok // TILES
    pairs = ((hidden, hidden_to), (gate, gate_to), (up, up_to))
    copies = [pltpu.make_async_copy(*pair, sem.at[i]) for i, pair in enumerate(pairs)]
    for copy in copies:
        copy.start()
    for t in range(TILES):
        span = slice(t * tile, (t + 1) * tile)
        made[span, :] = jnp.dot(
            onehot[span, :], landed[...], preferred_element_type=F32
        ).astype(BF16)
        copies.append(
            pltpu.make_async_copy(
                made.at[span], tokens_to.at[span], sem.at[len(pairs) + t]
            )
        )
        copies[-1].start()
    for copy in copies:
        copy.wait()


def shards(n_dp, n_g, tokens, gate_w, up_w, block_rows, block_count, route_gate, grad_hidden):
    n_blocks, block_len = block_rows.shape
    nb, blk = n_blocks * CUTS, block_len // CUTS
    n_tok, fw = tokens.shape
    w_rows, width = gate_w.shape
    routed_len = nb * blk
    depth = n_dp * w_rows
    n_bits = n_dp.bit_length() - 1
    factor = float((n_dp * routed_len) ** (-0.5))
    dma = pltpu.SemaphoreType.DMA
    vmem = pl.BlockSpec(memory_space=pltpu.VMEM)
    hbm = pl.BlockSpec(memory_space=pltpu.HBM)
    smem = pl.BlockSpec(memory_space=pltpu.SMEM)
    outs = (
        ((routed_len, width), BF16),
        ((w_rows, width), F32),
        ((w_rows, width), F32),
        ((n_tok, routed_len), BF16),
        ((routed_len, fw), BF16),
    )
    kept = sum(shape[0] * shape[1] * jnp.dtype(kind).itemsize for shape, kind in outs)
    made = pl.pallas_call(
        functools.partial(kernel, n_dp, n_g, factor),
        out_shape=tuple(pltpu.VMEM(shape, kind) for shape, kind in outs),
        in_specs=[hbm] * 4 + [smem] + [hbm] * 2,
        out_specs=(vmem,) * len(outs),
        scratch_shapes=[
            pltpu.VMEM((n_tok, fw), BF16),
            pltpu.VMEM((n_blocks, block_len), jnp.int32),
            pltpu.VMEM((n_blocks, block_len), F32),
            pltpu.VMEM((routed_len, width), BF16),
            pltpu.VMEM((routed_len, block_len), F32),
            pltpu.VMEM((n_g, routed_len, fw), BF16),
            pltpu.VMEM((depth, width), BF16),
            pltpu.VMEM((depth, width), BF16),
            pltpu.VMEM((routed_len, 2 * width), BF16),
            pltpu.VMEM((nb, n_g, blk, fw), F32),
            pltpu.VMEM((nb, n_g, blk, fw), BF16),
            pltpu.VMEM((nb, n_g, blk, fw), BF16),
            pltpu.VMEM((nb, n_g, blk, fw), BF16),
            pltpu.VMEM((depth, width), F32),
            pltpu.VMEM((depth, width), F32),
            pltpu.VMEM((depth, width), BF16),
            pltpu.VMEM((depth, width), BF16),
            pltpu.VMEM((depth, width), BF16),
            pltpu.VMEM((depth, width), BF16),
            dma((nb, 2)),
            dma((nb, n_g)),
            dma((nb, n_g)),
            dma((2, n_bits, n_bits)),
            dma((2, n_bits, n_bits)),
            dma((nb, n_g)),
            dma((nb, n_g)),
            dma((nb, n_g)),
            dma((2, n_bits, 4)),
            dma((2, n_bits, 4)),
            dma((6,)),
        ],
        compiler_params=pltpu.CompilerParams(
            collective_id=0, has_side_effects=True, vmem_limit_bytes=67043328 - kept
        ),
    )(tokens, gate_w, up_w, block_rows, block_count, route_gate, grad_hidden)
    return pl.pallas_call(
        store,
        out_shape=(
            jax.ShapeDtypeStruct((routed_len, width), BF16),
            jax.ShapeDtypeStruct((n_tok, fw), BF16),
            jax.ShapeDtypeStruct((w_rows, width), F32),
            jax.ShapeDtypeStruct((w_rows, width), F32),
        ),
        in_specs=[vmem] * len(outs),
        out_specs=(hbm,) * 4,
        scratch_shapes=[pltpu.VMEM((n_tok, fw), BF16), dma((3 + TILES,))],
        compiler_params=pltpu.CompilerParams(vmem_limit_bytes=8 * 2**20),
    )(*made)


def solution(mesh):
    return jax.shard_map(
        functools.partial(shards, mesh.shape["dp"], mesh.shape["group"]),
        mesh=mesh,
        in_specs=(
            P("dp", "group"),
            P("dp", "group"),
            P("dp", "group"),
            P("dp", None),
            P("dp"),
            P("dp", None),
            P("dp", "group"),
        ),
        out_specs=(P("dp", "group"), P("dp", "group"), P("dp", "group"), P("dp", "group")),
        check_vma=False,
    )
```
